32 devices in a mesh: row: 8 (over z, y), col: 4 (over x, core).
Axes of the slice: x: 2, y: 2, z: 4, core: 2. Of those that a mesh axis runs over, the one named last changes fastest.
Arguments:
- rhs: float32 [32768, 256], P(('row', 'col')), may hold values from -6 to 6
- local_mat: bfloat16 [32768, 1024], P(('row', 'col')), may hold values from -1 to 5
- local_inv: bfloat16 [32768, 1024], P(('row', 'col')), may hold values from -1 to 1
- basis_t: bfloat16 [3072, 1024], P(('row', 'col')), may hold values from -0.1875 to 0.1875
- coarse_inv: bfloat16 [3072, 3072], P('col', 'row'), may hold values from -0.109375 to 0.109375
- couple: float32 [32, 4, 128], P(('row', 'col')), may hold values from 0.5 to 2
- margin_rows: int32 [32, 4, 128], P(('row', 'col')), may hold values from 0 to 1023, as said below
Outputs:
- solution: float32 [32768, 256], P(('row', 'col'))
- residual: float32 [32768, 256], P(('row', 'col'))
The draws below stay inside these ranges and needn't reach their ends.
Inputs may be any that keep to these rules, and one draw needn't show every extreme that they name: `margin_rows`: within each subdomain the 512 listed rows are all different.
All inputs are finite; a program needn't handle non-finite values.
Results may differ from the reference program's by a relative error of at most 0.024.
Values may be sent and summed in bfloat16 or wider, within the bound.
No kernel may reach another device: no remote copies, remote signals or barrier semaphores. Data moves between devices by JAX's collectives and lax.ppermute only.
A program may use at most 64 MiB of HBM per device.

```python
import math
import jax
import jax.numpy as jnp
from jax import lax

NLOC = 1024
CPD = 96
NRHS = 256
OVL = 128
STEPS = 2
SUBDOMAINS = 32
COARSE = 3072
N_ROW = 8
N_COL = 4


def dominant_blocks(key, low, high, spread):
    diagonal = jax.random.uniform(jax.random.fold_in(key, 11), (SUBDOMAINS, NLOC, 1), jnp.float32, low, high)
    spread_part = jax.random.normal(jax.random.fold_in(key, 13), (SUBDOMAINS, NLOC, NLOC), jnp.float32) * (spread / math.sqrt(NLOC))
    matrix = spread_part + diagonal * jnp.eye(NLOC, dtype=jnp.float32)
    return matrix.reshape(SUBDOMAINS * NLOC, NLOC).astype(jnp.bfloat16)


def draw_local_mat(key, part):
    return dominant_blocks(jax.random.fold_in(key, 21), 2.0, 4.0, 0.8)


def draw_local_inv(key, part):
    return dominant_blocks(jax.random.fold_in(key, 22), 0.25, 0.5, 0.12)


def draw_margin_rows(key, part):
    subkeys = jax.random.split(jax.random.fold_in(key, 23), SUBDOMAINS)
    orders = jax.vmap(lambda one_key: jax.random.permutation(one_key, NLOC))(subkeys)
    return orders[:, :4 * OVL].reshape(SUBDOMAINS, 4, OVL).astype(jnp.int32)


def block_scale(rng, shape, cuts, smallest, largest):
    loudness = 1.0
    for axis_at, blocks in cuts:
        heights = jax.random.uniform(jax.random.fold_in(jax.random.fold_in(rng, 6), axis_at), (blocks,), jnp.float32, smallest / len(cuts), largest / len(cuts))
        loudness = loudness * jnp.repeat(jnp.exp(heights), shape[axis_at] // blocks).reshape((-1,) + (1,) * (len(shape) - 1 - axis_at))
    return loudness


def bell_draw(own_key, dims, scale, most, pieces=(), held_as=jnp.bfloat16):
    entries = jax.random.normal(own_key, dims, jnp.float32) * scale
    if len(pieces) > 0:
        entries = block_scale(own_key, dims, pieces, -0.22, 0.18) * entries
    return jnp.clip(entries, min=-most, max=most).astype(held_as)


def setup_inputs(seed: int = 0) -> dict:
    key_of = jax.random.split(jax.random.key(seed), 8)
    rhs = bell_draw(key_of[0], (SUBDOMAINS * NLOC, NRHS), 1.0, 6.0, ((0, 32),), jnp.float32)
    local_mat = draw_local_mat(jax.random.fold_in(key_of[7], 71), 0)
    local_inv = draw_local_inv(jax.random.fold_in(key_of[7], 71), 0)
    basis_t = bell_draw(key_of[3], (COARSE, NLOC), NLOC ** -0.5, 0.1875, ((0, 32),))
    coarse_inv = bell_draw(key_of[4], (COARSE, COARSE), COARSE ** -0.5, 0.109375, ((0, 4), (1, 8)))
    couple = jnp.clip(0.5 + 1.5 * jax.random.uniform(key_of[5], (SUBDOMAINS, 4, OVL), jnp.float32) ** block_scale(key_of[5], (SUBDOMAINS, 4, OVL), ((0, 32),), -0.2, 0.2), 0.5, 2.0)
    margin_rows = draw_margin_rows(jax.random.fold_in(key_of[7], 71), 0)
    return dict(rhs=rhs, local_mat=local_mat, local_inv=local_inv, basis_t=basis_t, coarse_inv=coarse_inv, couple=couple, margin_rows=margin_rows)


def apply_operator(vector, local_mat, couple, margin_rows):
    vector_b = vector.astype(jnp.bfloat16).reshape(SUBDOMAINS, NLOC, NRHS)
    face_vals = jax.vmap(lambda block, rows_of: block[rows_of])(vector_b, margin_rows)
    face_grid = face_vals.reshape(N_ROW, N_COL, 4, OVL, NRHS)
    padded = jnp.pad(face_grid, ((1, 1), (1, 1), (0, 0), (0, 0), (0, 0)))
    from_north = padded[:-2, 1:-1, 1]
    from_south = padded[2:, 1:-1, 0]
    from_west = padded[1:-1, :-2, 3]
    from_east = padded[1:-1, 2:, 2]
    received = jnp.stack([from_north, from_south, from_west, from_east], axis=2)
    received = received.reshape(SUBDOMAINS, 4, OVL, NRHS).astype(jnp.float32)
    coupling_terms = couple[:, :, :, None] * received

    def scatter_one(rows_of, values):
        return jnp.zeros((NLOC, NRHS), jnp.float32).at[rows_of.reshape(-1)].add(values.reshape(-1, NRHS))

    coupled = jax.vmap(scatter_one)(margin_rows, coupling_terms)
    matrices = local_mat.reshape(SUBDOMAINS, NLOC, NLOC)
    product = lax.map(lambda pair: jnp.dot(pair[0], pair[1], preferred_element_type=jnp.float32), (matrices, vector_b))
    return (product - coupled).reshape(SUBDOMAINS * NLOC, NRHS)


def coarse_correction(residual, basis_t, coarse_inv):
    rounded = residual.astype(jnp.bfloat16).reshape(SUBDOMAINS, NLOC, NRHS)
    basis = basis_t.reshape(SUBDOMAINS, CPD, NLOC)
    restricted = lax.map(lambda pair: jnp.dot(pair[0], pair[1], preferred_element_type=jnp.float32), (basis, rounded))
    restricted = restricted.astype(jnp.bfloat16).reshape(COARSE, NRHS)
    permuted = jnp.dot(coarse_inv, restricted, preferred_element_type=jnp.float32)
    coarse_part = permuted.reshape(N_COL, N_ROW, CPD, NRHS).transpose(1, 0, 2, 3).reshape(SUBDOMAINS, CPD, NRHS)
    coarse_b = coarse_part.astype(jnp.bfloat16)
    correction = lax.map(lambda pair: jnp.dot(pair[0].T, pair[1], preferred_element_type=jnp.float32), (basis, coarse_b))
    return correction.reshape(SUBDOMAINS * NLOC, NRHS)


def local_solve(residual, local_inv):
    rounded = residual.astype(jnp.bfloat16).reshape(SUBDOMAINS, NLOC, NRHS)
    inverses = local_inv.reshape(SUBDOMAINS, NLOC, NLOC)
    solved = lax.map(lambda pair: jnp.dot(pair[0], pair[1], preferred_element_type=jnp.float32), (inverses, rounded))
    return solved.reshape(SUBDOMAINS * NLOC, NRHS)


def reference(rhs, local_mat, local_inv, basis_t, coarse_inv, couple, margin_rows):
    solution = jnp.zeros(rhs.shape, jnp.float32)
    residual = rhs
    for sweep in range(STEPS):
        if sweep > 0:
            residual = rhs - apply_operator(solution, local_mat, couple, margin_rows)
        solution = solution + coarse_correction(residual, basis_t, coarse_inv)
        residual = rhs - apply_operator(solution, local_mat, couple, margin_rows)
        solution = solution + local_solve(residual, local_inv)
    residual = rhs - apply_operator(solution, local_mat, couple, margin_rows)
    return solution, residual
```

```python
import functools

import jax
import jax.numpy as jnp
from jax import lax
from jax.experimental import pallas as pl
from jax.experimental.pallas import tpu as pltpu
from jax.sharding import PartitionSpec as P

STEPS = 2
BF = jnp.bfloat16
F32 = jnp.float32
VMEM = pl.BlockSpec(memory_space=pltpu.VMEM)
LIMIT = 24 << 20


def mm(a, b):
    return jnp.dot(a, b, preferred_element_type=F32)


def mm_tn(a, b):
    return lax.dot_general(a, b, (((0,), (0,)), ((), ())), preferred_element_type=F32)


def mm_nt(a, b):
    return lax.dot_general(a, b, (((1,), (1,)), ((), ())), preferred_element_type=F32)


def call(kernel, outs, *args, name, scratch=(), flops=0):
    nbytes = sum(a.size * a.dtype.itemsize for a in args)
    return pl.pallas_call(
        kernel,
        out_shape=[jax.ShapeDtypeStruct(s, d) for s, d in outs],
        in_specs=[VMEM] * len(args),
        out_specs=[VMEM] * len(outs),
        scratch_shapes=list(scratch),
        compiler_params=pltpu.CompilerParams(vmem_limit_bytes=LIMIT),
        cost_estimate=pl.CostEstimate(flops=flops, bytes_accessed=nbytes, transcendentals=0),
        name=name,
    )(*args)


def tiles(rows):
    return 256 if rows % 256 == 0 else rows


def per_device(nr, nc, rhs, local_mat, local_inv, basis_t, coarse_inv, couple, margin_rows):
    nloc, nrhs = rhs.shape
    cpd = basis_t.shape[0]
    ovl = margin_rows.shape[2]
    nf = 4 * ovl
    nz = nr // 2
    both = ("row", "col")

    def pairs(row_parity, col_parity):
        perm = {}
        for r in range(nr):
            for c in range(nc):
                if row_parity is not None:
                    o = r + 1 if r % 2 == row_parity else r - 1
                    other = (o, c) if 0 <= o < nr else (r, c ^ 1)
                else:
                    o = c + 1 if c % 2 == col_parity else c - 1
                    other = (r, o) if 0 <= o < nc else (r ^ 1, c)
                perm[r * nc + c] = other[0] * nc + other[1]
        return sorted(perm.items())

    slot_perms = [pairs(1, None), pairs(None, 1), pairs(0, None), pairs(None, 0)]

    def slot_faces():
        r, c = lax.axis_index("row"), lax.axis_index("col")
        pr, pc = lax.rem(r, 2), lax.rem(c, 2)
        one = lambda ok: jnp.where(ok, 1.0, 0.0).astype(F32)
        return [
            (pr, one((pr == 1) & (r + 1 < nr) | (pr == 0) & (r > 0))),
            (2 + pc, one((pc == 1) & (c + 1 < nc) | (pc == 0) & (c > 0))),
            (1 - pr, one((pr == 1) | (r + 1 < nr))),
            (3 - pc, one((pc == 1) | (c + 1 < nc))),
        ]

    def halo(faces):
        return [lax.ppermute(f, both, p) for f, p in zip(faces, slot_perms)]

    def k_setup(rows_ref, couple_ref, inv_ref, basis_ref, sel_ref, wt_ref, bf_ref, t_ref, m_ref, f_ref):
        for s, (k, ok) in enumerate(slot_faces()):
            row = rows_ref[0, pl.ds(k, 1), :]
            w = couple_ref[0, pl.ds(k, 1), :] * ok
            at = pl.ds(s * ovl, ovl)
            down = lax.broadcasted_iota(jnp.int32, (nloc, ovl), 0)
            wt_ref[:, at] = jnp.where(down == row, jnp.broadcast_to(w, (nloc, ovl)), 0.0).astype(BF)
            idx = jnp.broadcast_to(row.astype(F32), (ovl, ovl)).T
            for j in range(nloc // ovl):
                across = lax.broadcasted_iota(jnp.int32, (ovl, ovl), 1) + j * ovl
                sel_ref[at, pl.ds(j * ovl, ovl)] = jnp.where(idx == across.astype(F32), 1.0, 0.0).astype(BF)
        bf_ref[...] = mm_nt(sel_ref[...], basis_ref[...]).astype(BF)
        t_ref[...] = mm(basis_ref[...], wt_ref[...]).astype(BF)
        step = tiles(nloc)

        @pl.loop(0, nloc // step)
        def _(i):
            at = pl.ds(pl.multiple_of(i * step, step), step)
            m_ref[at, :] = mm(inv_ref[at, :], wt_ref[...]).astype(BF)

        f_ref[...] = mm(sel_ref[...], m_ref[...]).astype(BF)

    sel, wt, bfac, tmat, mmat, fmat = call(
        k_setup,
        [((nf, nloc), BF), ((nloc, nf), BF), ((nf, cpd), BF), ((cpd, nf), BF), ((nloc, nf), BF), ((nf, nf), BF)],
        margin_rows, couple, local_inv, basis_t, name="setup", flops=2 * nloc * nf * (nloc + nf),
    )

    def k_restrict(rhs_ref, basis_ref, out_ref):
        out_ref[...] = mm(basis_ref[...], rhs_ref[...].astype(BF)).astype(BF)

    def k_coarse(*refs):
        blocks, (inv_ref, keep_ref, send_ref, group, prod) = refs[:nc], refs[nc:]
        r, c = lax.axis_index("row"), lax.axis_index("col")
        for i, block in enumerate(blocks):
            group[pl.ds(pl.multiple_of((c ^ i) * cpd, 16), cpd), :] = block[...]
        prod[...] = mm(inv_ref[...], group[...])
        for i in range(nz):
            for ref, m in ((keep_ref, 2 * i), (send_ref, 2 * i + 1)):
                src = pl.ds(pl.multiple_of((r ^ m) * cpd, 8), cpd)
                ref[pl.ds(i * cpd, cpd), :] = prod[src, :].astype(ref.dtype)

    def k_half(keep_ref, recv_ref, own_ref, *sends):
        own_ref[...] = keep_ref[pl.ds(0, cpd), :] + recv_ref[pl.ds(0, cpd), :].astype(F32)
        for i, ref in enumerate(sends):
            at = pl.ds((i + 1) * cpd, cpd)
            ref[...] = (keep_ref[at, :] + recv_ref[at, :].astype(F32)).astype(BF)

    def coarse_parts(restricted):
        blocks = [restricted] + [
            lax.ppermute(restricted, "col", [(i, i ^ k) for i in range(nc)]) for k in range(1, nc)
        ]
        keep, send = call(
            k_coarse, [((nz * cpd, nrhs), F32), ((nz * cpd, nrhs), BF)], *blocks, coarse_inv,
            scratch=[pltpu.VMEM((nc * cpd, nrhs), BF), pltpu.VMEM((nr * cpd, nrhs), F32)],
            name="coarse", flops=2 * nr * cpd * nc * cpd * nrhs,
        )
        recv = lax.ppermute(send, "row", [(i, i ^ 1) for i in range(nr)])
        own, *sends = call(
            k_half, [((cpd, nrhs), F32)] + [((cpd, nrhs), BF)] * (nz - 1), keep, recv, name="half",
        )
        recvs = [
            lax.ppermute(s, "row", [(i, i ^ (2 * (k + 1))) for i in range(nr)]) for k, s in enumerate(sends)
        ]
        return [own] + recvs

    def k_coarse_faces(*refs):
        parts, (bf_ref, y_ref), faces = refs[:nz], refs[nz : nz + 2], refs[nz + 2 :]
        total = parts[0][...]
        for p in parts[1:]:
            total = total + p[...].astype(F32)
        y = total.astype(BF)
        y_ref[...] = y
        for s, ref in enumerate(faces):
            ref[...] = mm(bf_ref[pl.ds(s * ovl, ovl), :], y).astype(BF)

    def coarse_faces(parts):
        y, *faces = call(
            k_coarse_faces, [((cpd, nrhs), BF)] + [((ovl, nrhs), BF)] * 4, *parts, bfac, name="coarse_faces",
        )
        return y, faces

    step = tiles(nloc)

    def row_loop(body):
        @pl.loop(0, nloc // step)
        def _(i):
            body(pl.ds(pl.multiple_of(i * step, step), step))

    def k_local(first, y_ref, basis_ref, base_ref, old_ref, mat_ref, inv_ref, sel_ref, sol_ref, face_ref, vb, wb):
        def corr_tile(at):
            corr = mm_tn(basis_ref[:, at], y_ref[...])
            vb[at, :] = corr.astype(BF)
            sol_ref[at, :] = corr if first else old_ref[at, :] + corr

        for i in range(nloc // step):
            corr_tile(pl.ds(i * step, step))

        def res_tile(at):
            wb[at, :] = (base_ref[at, :] - mm(mat_ref[at, :], vb[...])).astype(BF)

        row_loop(res_tile)

        def sol_tile(at):
            sol = sol_ref[at, :] + mm(inv_ref[at, :], wb[...])
            sol_ref[at, :] = sol
            vb[at, :] = sol.astype(BF)

        row_loop(sol_tile)
        face_ref[...] = mm(sel_ref[...], vb[...])

    def local(y, base, old, first):
        args = (y, basis_t, base) + (() if first else (old,)) + (local_mat, local_inv, sel)
        body = functools.partial(k_local, first)
        if first:
            kernel = lambda a, b, c, *rest: body(a, b, c, None, *rest)
        else:
            kernel = body
        return call(
            kernel, [((nloc, nrhs), F32), ((nf, nrhs), F32)], *args,
            scratch=[pltpu.VMEM((nloc, nrhs), BF)] * 2, name="local", flops=5 * nloc * nloc * nrhs,
        )

    def k_faces(base_ref, f_ref, *refs):
        recvs, faces = refs[:4], refs[4:]
        recv = jnp.concatenate([x[...] for x in recvs], axis=0)
        for s, ref in enumerate(faces):
            at = pl.ds(s * ovl, ovl)
            ref[...] = (base_ref[at, :] + mm(f_ref[at, :], recv)).astype(BF)

    def faces_after(base, recv):
        return call(k_faces, [((ovl, nrhs), BF)] * 4, base, fmat, *recv, name="faces", flops=2 * nf * nf * nrhs)

    def k_advance(restrict, sol_ref, m_ref, rhs_ref, mat_ref, basis_ref, *refs):
        recvs, (new_ref, res_ref), rest = refs[:4], refs[4:6], refs[6:]
        recv, vb = rest[-2:]
        for s, x in enumerate(recvs):
            recv[pl.ds(s * ovl, ovl), :] = x[...]

        def sol_tile(at):
            new = sol_ref[at, :] + mm(m_ref[at, :], recv[...])
            new_ref[at, :] = new
            vb[at, :] = new.astype(BF)

        row_loop(sol_tile)

        def res_tile(at):
            res_ref[at, :] = rhs_ref[at, :] - mm(mat_ref[at, :], vb[...])

        row_loop(res_tile)
        if restrict:
            rest[0][...] = mm(basis_ref[...], res_ref[...].astype(BF))

    def advance(sol, recv, restrict):
        outs = [((nloc, nrhs), F32)] * 2 + ([((cpd, nrhs), F32)] if restrict else [])
        return call(
            functools.partial(k_advance, restrict), outs, sol, mmat, rhs, local_mat, basis_t, *recv,
            scratch=[pltpu.VMEM((nf, nrhs), BF), pltpu.VMEM((nloc, nrhs), BF)],
            name="advance", flops=3 * nloc * nloc * nrhs,
        )

    def k_restrict_recv(base_ref, t_ref, *refs):
        recvs, out_ref = refs[:4], refs[4]
        recv = jnp.concatenate([x[...] for x in recvs], axis=0)
        out_ref[...] = (base_ref[...] + mm(t_ref[...], recv)).astype(BF)

    def k_couple(res_ref, wt_ref, *refs):
        recvs, out_ref, recv = refs[:4], refs[4], refs[5]
        for s, x in enumerate(recvs):
            recv[pl.ds(s * ovl, ovl), :] = x[...]

        def tile(at):
            out_ref[at, :] = res_ref[at, :] + mm(wt_ref[at, :], recv[...])

        row_loop(tile)

    def coupled(res, recv):
        return call(
            k_couple, [((nloc, nrhs), F32)], res, wt, *recv,
            scratch=[pltpu.VMEM((nf, nrhs), BF)], name="couple", flops=2 * nloc * nf * nrhs,
        )[0]

    (restricted,) = call(k_restrict, [((cpd, nrhs), BF)], rhs, basis_t, name="restrict")
    residual, solution = rhs, None
    for sweep in range(STEPS):
        y, faces = coarse_faces(coarse_parts(restricted))
        recv = halo(faces)
        partial, face_base = local(y, residual, solution, sweep == 0)
        recv2 = halo(faces_after(face_base, recv))
        last = sweep == STEPS - 1
        if last:
            solution, res = advance(partial, recv, False)
        else:
            solution, res, restr = advance(partial, recv, True)
            (restricted,) = call(
                k_restrict_recv, [((cpd, nrhs), BF)], restr, tmat, *recv2, name="restrict_recv",
            )
        residual = coupled(res, recv2)
    return (solution, residual)


def solution(mesh):
    nr, nc = mesh.shape["row"], mesh.shape["col"]
    placed = (
        P(("row", "col"), None),
        P(("row", "col"), None),
        P(("row", "col"), None),
        P(("row", "col"), None),
        P("col", "row"),
        P(("row", "col"), None, None),
        P(("row", "col"), None, None),
    )
    return jax.shard_map(
        functools.partial(per_device, nr, nc),
        mesh=mesh,
        in_specs=placed,
        out_specs=(P(("row", "col"), None), P(("row", "col"), None)),
        check_vma=False,
    )
```

```python
import functools

import jax
import jax.numpy as jnp
from jax import lax
from jax.experimental import pallas as pl
from jax.experimental.pallas import tpu as pltpu
from jax.sharding import PartitionSpec as P

STEPS = 2
BF = jnp.bfloat16
F32 = jnp.float32
VMEM = pl.BlockSpec(memory_space=pltpu.VMEM)
ANY = pl.BlockSpec(memory_space=pl.ANY)
LIMIT = 24 << 20


def mm(a, b):
    return jnp.dot(a, b, preferred_element_type=F32)


def call(kernel, outs, *args, name, scratch=(), flops=0, hbm_ins=0, hbm_outs=0, tokens=0):
    nbytes = sum(a.size * a.dtype.itemsize for a in args)
    inner = len(args) - hbm_ins - tokens
    return pl.pallas_call(
        kernel,
        out_shape=[jax.ShapeDtypeStruct(s, d) for s, d in outs],
        in_specs=[ANY] * hbm_ins + [VMEM] * inner + [ANY] * tokens,
        out_specs=[ANY] * hbm_outs + [VMEM] * (len(outs) - hbm_outs),
        scratch_shapes=list(scratch),
        compiler_params=pltpu.CompilerParams(vmem_limit_bytes=LIMIT),
        cost_estimate=pl.CostEstimate(flops=flops, bytes_accessed=nbytes, transcendentals=0),
        name=name,
    )(*args)


def tiles(rows):
    return 256 if rows % 256 == 0 else rows


def per_device(nr, nc, rhs, local_mat, local_inv, basis_t, coarse_inv, couple, margin_rows):
    nloc, nrhs = rhs.shape
    cpd = basis_t.shape[0]
    ovl = margin_rows.shape[2]
    nf = 4 * ovl
    nz = nr // 2
    both = ("row", "col")

    step = tiles(nloc)

    def row_loop(body):
        @pl.loop(0, nloc // step)
        def _(i):
            body(pl.ds(pl.multiple_of(i * step, step), step))

    def pairs(row_parity, col_parity):
        perm = {}
        for r in range(nr):
            for c in range(nc):
                if row_parity is not None:
                    o = r + 1 if r % 2 == row_parity else r - 1
                    other = (o, c) if 0 <= o < nr else (r, c ^ 1)
                else:
                    o = c + 1 if c % 2 == col_parity else c - 1
                    other = (r, o) if 0 <= o < nc else (r ^ 1, c)
                perm[r * nc + c] = other[0] * nc + other[1]
        return sorted(perm.items())

    slot_perms = [pairs(1, None), pairs(None, 1), pairs(0, None), pairs(None, 0)]

    def slot_faces():
        r, c = lax.axis_index("row"), lax.axis_index("col")
        pr, pc = lax.rem(r, 2), lax.rem(c, 2)
        one = lambda ok: jnp.where(ok, 1.0, 0.0).astype(F32)
        return [
            (pr, one((pr == 1) & (r + 1 < nr) | (pr == 0) & (r > 0))),
            (2 + pc, one((pc == 1) & (c + 1 < nc) | (pc == 0) & (c > 0))),
            (1 - pr, one((pr == 1) | (r + 1 < nr))),
            (3 - pc, one((pc == 1) | (c + 1 < nc))),
        ]

    def halo(faces):
        return [lax.ppermute(f, both, p) for f, p in zip(faces, slot_perms)]

    def k_select(inv_hbm, table_ref, token, sel_ref, wt_ref, inv_ref, sem):
        load = pltpu.make_async_copy(inv_hbm, inv_ref, sem)
        load.start()
        for s, (k, ok) in enumerate(slot_faces()):
            row = table_ref[pl.ds(k, 1), :].astype(jnp.int32)
            w = table_ref[pl.ds(4 + k, 1), :] * ok
            at = pl.ds(s * ovl, ovl)
            down = lax.broadcasted_iota(jnp.int32, (nloc, ovl), 0)
            wt_ref[:, at] = jnp.where(down == row, jnp.broadcast_to(w, (nloc, ovl)), 0.0).astype(BF)
            idx = jnp.broadcast_to(row.astype(F32), (ovl, ovl)).T
            for j in range(nloc // ovl):
                across = lax.broadcasted_iota(jnp.int32, (ovl, ovl), 1) + j * ovl
                sel_ref[at, pl.ds(j * ovl, ovl)] = jnp.where(idx == across.astype(F32), 1.0, 0.0).astype(BF)
        load.wait()

    def k_products(
        sel_ref, wt_ref, inv_ref, mat_ref, basis_ref, token, bf_ref, t_ref, si_ref, f_ref, bt_ref, lb_ref
    ):
        bt = basis_ref[...].astype(F32).T.astype(BF)
        bt_ref[...] = bt
        bf_ref[...] = mm(sel_ref[...], bt).astype(BF)
        t_ref[...] = mm(basis_ref[...], wt_ref[...]).astype(BF)
        fstep = tiles(nf)

        @pl.loop(0, nf // fstep)
        def _(i):
            at = pl.ds(pl.multiple_of(i * fstep, fstep), fstep)
            si_ref[at, :] = mm(sel_ref[at, :], inv_ref[...]).astype(BF)
            f_ref[at, :] = mm(si_ref[at, :], wt_ref[...]).astype(BF)

        def tile(at):
            lb_ref[at, :] = mm(mat_ref[at, :], bt_ref[...]).astype(BF)

        row_loop(tile)

    def k_coarse(*refs):
        blocks, (inv_ref, keep_ref, send_ref, group, prod) = refs[:nc], refs[nc:]
        r, c = lax.axis_index("row"), lax.axis_index("col")
        for i, block in enumerate(blocks):
            group[pl.ds(pl.multiple_of((c ^ i) * cpd, 16), cpd), :] = block[...]
        prod[...] = mm(inv_ref[...], group[...])
        for i in range(nz):
            for ref, m in ((keep_ref, 2 * i), (send_ref, 2 * i + 1)):
                src = pl.ds(pl.multiple_of((r ^ m) * cpd, 8), cpd)
                ref[pl.ds(i * cpd, cpd), :] = prod[src, :].astype(ref.dtype)

    def k_half(keep_ref, recv_ref, token, own_ref, *sends):
        own_ref[...] = keep_ref[pl.ds(0, cpd), :] + recv_ref[pl.ds(0, cpd), :].astype(F32)
        for i, ref in enumerate(sends):
            at = pl.ds((i + 1) * cpd, cpd)
            ref[...] = (keep_ref[at, :] + recv_ref[at, :].astype(F32)).astype(BF)

    def coarse_send(restricted, inv):
        blocks = [restricted] + [
            lax.ppermute(restricted, "col", [(i, i ^ k) for i in range(nc)]) for k in range(1, nc)
        ]
        keep, send = call(
            k_coarse, [((nz * cpd, nrhs), F32), ((nz * cpd, nrhs), BF)], *blocks, inv,
            scratch=[pltpu.VMEM((nc * cpd, nrhs), BF), pltpu.VMEM((nr * cpd, nrhs), F32)],
            name="coarse", flops=2 * nr * cpd * nc * cpd * nrhs,
        )
        return keep, lax.ppermute(send, "row", [(i, i ^ 1) for i in range(nr)])

    def coarse_recv(keep, recv, token):
        own, *sends = call(
            k_half, [((cpd, nrhs), F32)] + [((cpd, nrhs), BF)] * (nz - 1), keep, recv, token,
            tokens=1, name="half",
        )
        recvs = [
            lax.ppermute(s, "row", [(i, i ^ (2 * (k + 1))) for i in range(nr)]) for k, s in enumerate(sends)
        ]
        return [own] + recvs

    def k_coarse_faces(*refs):
        parts, (bf_ref, y_ref), faces = refs[:nz], refs[nz : nz + 2], refs[nz + 2 :]
        total = parts[0][...]
        for p in parts[1:]:
            total = total + p[...].astype(F32)
        y = total.astype(BF)
        y_ref[...] = y
        for s, ref in enumerate(faces):
            ref[...] = mm(bf_ref[pl.ds(s * ovl, ovl), :], y).astype(BF)

    def coarse_faces(parts):
        y, *faces = call(
            k_coarse_faces, [((cpd, nrhs), BF)] + [((ovl, nrhs), BF)] * 4, *parts, bfac, name="coarse_faces",
        )
        return y, faces

    def k_local(y_ref, base_ref, lb_ref, si_ref, bf_ref, *refs):
        olds, face_ref, wb = refs[:-2], refs[-2], refs[-1]
        y = y_ref[...]

        def tile(at):
            wb[at, :] = (base_ref[at, :] - mm(lb_ref[at, :], y)).astype(BF)

        row_loop(tile)
        for s in range(4):
            at = pl.ds(s * ovl, ovl)
            face = mm(bf_ref[at, :], y) + mm(si_ref[at, :], wb[...])
            face_ref[at, :] = face + olds[s][...].astype(F32) if olds else face

    def local(y, base, olds):
        (face,) = call(
            k_local, [((nf, nrhs), F32)], y, base, lbmat, simat, bfac, *olds,
            scratch=[pltpu.VMEM((nloc, nrhs), BF)], name="local", flops=2 * nf * nloc * nrhs,
        )
        return face

    def k_faces(base_ref, f_ref, *refs):
        recvs, faces = refs[:4], refs[4:]
        recv = jnp.concatenate([x[...] for x in recvs], axis=0)
        for s, ref in enumerate(faces):
            at = pl.ds(s * ovl, ovl)
            ref[...] = (base_ref[at, :] + mm(f_ref[at, :], recv)).astype(BF)

    def faces_after(base, recv):
        return call(k_faces, [((ovl, nrhs), BF)] * 4, base, fmat, *recv, name="faces", flops=2 * nf * nf * nrhs)

    def k_advance(first, last, *refs):
        y_ref, base_ref, lb_ref, bt_ref, wt_ref, inv_ref, mat_ref, rhs_ref, basis_ref = refs[:9]
        recvs, refs = refs[9:13], refs[13:]
        old_ref, refs = (None, refs) if first else (refs[0], refs[1:])
        out_ref, res_ref = refs[:2]
        if last:
            wb, vb, recv, new_ref, sem = refs[2:]
        else:
            restr_ref, wb, vb, recv = refs[2:]
            new_ref = out_ref
        y = y_ref[...]
        for s, x in enumerate(recvs):
            recv[pl.ds(s * ovl, ovl), :] = x[...]

        def base_tile(at):
            wb[at, :] = (base_ref[at, :] - mm(lb_ref[at, :], y) + mm(wt_ref[at, :], recv[...])).astype(BF)

        row_loop(base_tile)

        def sol_tile(at):
            new = mm(bt_ref[at, :], y) + mm(inv_ref[at, :], wb[...])
            if not first:
                new = new + old_ref[at, :]
            new_ref[at, :] = new
            vb[at, :] = new.astype(BF)

        row_loop(sol_tile)
        if last:
            store = pltpu.make_async_copy(new_ref, out_ref, sem)
            store.start()

        def res_tile(at):
            res_ref[at, :] = rhs_ref[at, :] - mm(mat_ref[at, :], vb[...])

        row_loop(res_tile)
        if last:
            store.wait()
        else:
            restr_ref[...] = mm(basis_ref[...], res_ref[...].astype(BF))

    def advance(y, base, recv, old, last):
        first = old is None
        outs = [((nloc, nrhs), F32)] * 2 + ([] if last else [((cpd, nrhs), F32)])
        extra = [pltpu.VMEM((nloc, nrhs), F32), pltpu.SemaphoreType.DMA] if last else []
        return call(
            functools.partial(k_advance, first, last), outs,
            y, base, lbmat, btmat, wt, local_inv, local_mat, rhs, basis_t, *recv, *([] if first else [old]),
            scratch=[pltpu.VMEM((nloc, nrhs), BF)] * 2 + [pltpu.VMEM((nf, nrhs), BF)] + extra,
            hbm_outs=1 if last else 0, name="advance", flops=5 * nloc * nloc * nrhs,
        )

    def k_restrict_recv(base_ref, t_ref, *refs):
        recvs, out_ref = refs[:4], refs[4]
        recv = jnp.concatenate([x[...] for x in recvs], axis=0)
        out_ref[...] = (base_ref[...] + mm(t_ref[...], recv)).astype(BF)

    def k_couple(res_ref, wt_ref, *refs):
        recvs, out_ref, recv = refs[:4], refs[4], refs[5]
        for s, x in enumerate(recvs):
            recv[pl.ds(s * ovl, ovl), :] = x[...]

        def tile(at):
            out_ref[at, :] = res_ref[at, :] + mm(wt_ref[at, :], recv[...])

        row_loop(tile)

    def k_couple_last(res_ref, wt_ref, *refs):
        recvs, (out_ref, recv, buf, sems) = refs[:4], refs[4:]
        for s, x in enumerate(recvs):
            recv[pl.ds(s * ovl, ovl), :] = x[...]
        copies = []
        for i in range(nloc // step):
            at = pl.ds(i * step, step)
            buf[at, :] = res_ref[at, :] + mm(wt_ref[at, :], recv[...])
            copies.append(pltpu.make_async_copy(buf.at[at, :], out_ref.at[at, :], sems.at[i]))
            copies[-1].start()
        for copy in copies:
            copy.wait()

    def coupled(res, recv, last):
        extra = [pltpu.VMEM((nloc, nrhs), F32), pltpu.SemaphoreType.DMA((nloc // step,))] if last else []
        return call(
            k_couple_last if last else k_couple, [((nloc, nrhs), F32)], res, wt, *recv,
            scratch=[pltpu.VMEM((nf, nrhs), BF)] + extra, hbm_outs=1 if last else 0,
            name="couple", flops=2 * nloc * nf * nrhs,
        )[0]

    restricted = mm(basis_t, rhs.astype(BF)).astype(BF)
    table = jnp.concatenate([margin_rows[0].astype(F32), couple[0]], axis=0)
    sel, wt, inv_here = call(
        k_select, [((nf, nloc), BF), ((nloc, nf), BF), (coarse_inv.shape, BF)],
        coarse_inv, table, restricted, hbm_ins=1, tokens=1, name="select",
        scratch=[pltpu.SemaphoreType.DMA],
    )
    keep, recv = coarse_send(restricted, inv_here)
    bfac, tmat, simat, fmat, btmat, lbmat = call(
        k_products,
        [((nf, cpd), BF), ((cpd, nf), BF), ((nf, nloc), BF), ((nf, nf), BF), ((nloc, cpd), BF), ((nloc, cpd), BF)],
        sel, wt, local_inv, local_mat, basis_t, keep, tokens=1,
        name="products", flops=2 * nf * nloc * (nloc + nf + 3 * cpd),
    )
    token = tmat
    residual, solution, sent = rhs, None, []
    for sweep in range(STEPS):
        y, faces = coarse_faces(coarse_recv(keep, recv, token))
        recv = halo(faces)
        sent = faces_after(local(y, residual, sent), recv)
        recv2 = halo(sent)
        last = sweep == STEPS - 1
        new = advance(y, residual, recv, solution, last)
        solution, res = new[:2]
        if not last:
            (restricted,) = call(
                k_restrict_recv, [((cpd, nrhs), BF)], new[2], tmat, *recv2, name="restrict_recv",
            )
            keep, recv = coarse_send(restricted, inv_here)
        residual = coupled(res, recv2, last)
        token = residual
    return (solution, residual)


def solution(mesh):
    nr, nc = mesh.shape["row"], mesh.shape["col"]
    placed = (
        P(("row", "col"), None),
        P(("row", "col"), None),
        P(("row", "col"), None),
        P(("row", "col"), None),
        P("col", "row"),
        P(("row", "col"), None, None),
        P(("row", "col"), None, None),
    )
    return jax.shard_map(
        functools.partial(per_device, nr, nc),
        mesh=mesh,
        in_specs=placed,
        out_specs=(P(("row", "col"), None), P(("row", "col"), None)),
        check_vma=False,
    )
```

```python
import functools

import jax
import jax.numpy as jnp
from jax import lax
from jax.experimental import pallas as pl
from jax.experimental.pallas import tpu as pltpu
from jax.sharding import PartitionSpec as P

STEPS = 2
BF = jnp.bfloat16
F32 = jnp.float32
VMEM = pl.BlockSpec(memory_space=pltpu.VMEM)
ANY = pl.BlockSpec(memory_space=pl.ANY)
LIMIT = 24 << 20


def mm(a, b):
    return jnp.dot(a, b, preferred_element_type=F32)


def call(kernel, outs, *args, name, scratch=(), flops=0, hbm_ins=0, hbm_outs=0, tokens=0):
    nbytes = sum(a.size * a.dtype.itemsize for a in args)
    inner = len(args) - hbm_ins - tokens
    return pl.pallas_call(
        kernel,
        out_shape=[jax.ShapeDtypeStruct(s, d) for s, d in outs],
        in_specs=[ANY] * hbm_ins + [VMEM] * inner + [ANY] * tokens,
        out_specs=[ANY] * hbm_outs + [VMEM] * (len(outs) - hbm_outs),
        scratch_shapes=list(scratch),
        compiler_params=pltpu.CompilerParams(vmem_limit_bytes=LIMIT),
        cost_estimate=pl.CostEstimate(flops=flops, bytes_accessed=nbytes, transcendentals=0),
        name=name,
    )(*args)


def tiles(rows, most=512):
    return most if rows % most == 0 else rows


def per_device(nr, nc, rhs, local_mat, local_inv, basis_t, coarse_inv, couple, margin_rows):
    nloc, nrhs = rhs.shape
    cpd = basis_t.shape[0]
    ovl = margin_rows.shape[2]
    nf = 4 * ovl
    nz = nr // 2
    both = ("row", "col")

    step, last_step = tiles(nloc), tiles(nloc, 256)

    def row_loop(body):
        @pl.loop(0, nloc // step)
        def _(i):
            body(pl.ds(pl.multiple_of(i * step, step), step))

    def pairs(row_parity, col_parity):
        perm = {}
        for r in range(nr):
            for c in range(nc):
                if row_parity is not None:
                    o = r + 1 if r % 2 == row_parity else r - 1
                    other = (o, c) if 0 <= o < nr else (r, c ^ 1)
                else:
                    o = c + 1 if c % 2 == col_parity else c - 1
                    other = (r, o) if 0 <= o < nc else (r, nc - 1 - c)
                perm[r * nc + c] = other[0] * nc + other[1]
        return sorted(perm.items())

    slot_perms = [pairs(1, None), pairs(None, 1), pairs(0, None), pairs(None, 0)]

    def slot_faces():
        r, c = lax.axis_index("row"), lax.axis_index("col")
        pr, pc = lax.rem(r, 2), lax.rem(c, 2)
        one = lambda ok: jnp.where(ok, 1.0, 0.0).astype(F32)
        return [
            (pr, one((pr == 1) & (r + 1 < nr) | (pr == 0) & (r > 0))),
            (2 + pc, one((pc == 1) & (c + 1 < nc) | (pc == 0) & (c > 0))),
            (1 - pr, one((pr == 1) | (r + 1 < nr))),
            (3 - pc, one((pc == 1) | (c + 1 < nc))),
        ]

    def halo(faces):
        return [lax.ppermute(f, both, p) for f, p in zip(faces, slot_perms)]

    def k_select(inv_hbm, table_ref, token, sel_ref, wt_ref, inv_ref, sem):
        load = pltpu.make_async_copy(inv_hbm, inv_ref, sem)
        load.start()
        for s, (k, ok) in enumerate(slot_faces()):
            row = table_ref[pl.ds(k, 1), :].astype(jnp.int32)
            w = table_ref[pl.ds(4 + k, 1), :] * ok
            at = pl.ds(s * ovl, ovl)
            down = lax.broadcasted_iota(jnp.int32, (nloc, ovl), 0)
            wt_ref[:, at] = jnp.where(down == row, jnp.broadcast_to(w, (nloc, ovl)), 0.0).astype(BF)
            idx = jnp.broadcast_to(row.astype(F32), (ovl, ovl)).T
            for j in range(nloc // ovl):
                across = lax.broadcasted_iota(jnp.int32, (ovl, ovl), 1) + j * ovl
                sel_ref[at, pl.ds(j * ovl, ovl)] = jnp.where(idx == across.astype(F32), 1.0, 0.0).astype(BF)
        load.wait()

    def k_products(
        sel_ref, wt_ref, inv_ref, mat_ref, basis_ref, token, bf_ref, t_ref, si_ref, f_ref, bt_ref, lb_ref
    ):
        bt = basis_ref[...].astype(F32).T.astype(BF)
        bt_ref[...] = bt
        bf_ref[...] = mm(sel_ref[...], bt).astype(BF)
        t_ref[...] = mm(basis_ref[...], wt_ref[...]).astype(BF)
        fstep = tiles(nf)

        @pl.loop(0, nf // fstep)
        def _(i):
            at = pl.ds(pl.multiple_of(i * fstep, fstep), fstep)
            si_ref[at, :] = mm(sel_ref[at, :], inv_ref[...]).astype(BF)
            f_ref[at, :] = mm(si_ref[at, :], wt_ref[...]).astype(BF)

        def tile(at):
            lb_ref[at, :] = mm(mat_ref[at, :], bt_ref[...]).astype(BF)

        row_loop(tile)

    def k_coarse(*refs):
        blocks, (inv_ref, keep_ref, send_ref, group, prod) = refs[:nc], refs[nc:]
        r, c = lax.axis_index("row"), lax.axis_index("col")
        for i, block in enumerate(blocks):
            group[pl.ds(pl.multiple_of((c ^ i) * cpd, 16), cpd), :] = block[...]
        prod[...] = mm(inv_ref[...], group[...])
        for i in range(nz):
            for ref, m in ((keep_ref, 2 * i), (send_ref, 2 * i + 1)):
                src = pl.ds(pl.multiple_of((r ^ m) * cpd, 8), cpd)
                ref[pl.ds(i * cpd, cpd), :] = prod[src, :].astype(ref.dtype)

    def k_half(keep_ref, recv_ref, token, own_ref, *sends):
        own_ref[...] = keep_ref[pl.ds(0, cpd), :] + recv_ref[pl.ds(0, cpd), :].astype(F32)
        for i, ref in enumerate(sends):
            at = pl.ds((i + 1) * cpd, cpd)
            ref[...] = (keep_ref[at, :] + recv_ref[at, :].astype(F32)).astype(BF)

    def coarse_send(restricted, inv):
        blocks = [restricted] + [
            lax.ppermute(restricted, "col", [(i, i ^ k) for i in range(nc)]) for k in range(1, nc)
        ]
        keep, send = call(
            k_coarse, [((nz * cpd, nrhs), F32), ((nz * cpd, nrhs), BF)], *blocks, inv,
            scratch=[pltpu.VMEM((nc * cpd, nrhs), BF), pltpu.VMEM((nr * cpd, nrhs), F32)],
            name="coarse", flops=2 * nr * cpd * nc * cpd * nrhs,
        )
        return keep, lax.ppermute(send, "row", [(i, i ^ 1) for i in range(nr)])

    def coarse_recv(keep, recv, token):
        own, *sends = call(
            k_half, [((cpd, nrhs), F32)] + [((cpd, nrhs), BF)] * (nz - 1), keep, recv, token,
            tokens=1, name="half",
        )
        recvs = [
            lax.ppermute(s, "row", [(i, i ^ (2 * (k + 1))) for i in range(nr)]) for k, s in enumerate(sends)
        ]
        return [own] + recvs

    def k_coarse_faces(*refs):
        parts, (bf_ref, y_ref), faces = refs[:nz], refs[nz : nz + 2], refs[nz + 2 :]
        total = parts[0][...]
        for p in parts[1:]:
            total = total + p[...].astype(F32)
        y = total.astype(BF)
        y_ref[...] = y
        for s, ref in enumerate(faces):
            ref[...] = mm(bf_ref[pl.ds(s * ovl, ovl), :], y).astype(BF)

    def coarse_faces(parts):
        y, *faces = call(
            k_coarse_faces, [((cpd, nrhs), BF)] + [((ovl, nrhs), BF)] * 4, *parts, bfac, name="coarse_faces",
        )
        return y, faces

    def k_local(y_ref, base_ref, lb_ref, si_ref, bf_ref, *refs):
        olds, face_ref, wb = refs[:-2], refs[-2], refs[-1]
        y = y_ref[...]

        def tile(at):
            wb[at, :] = (base_ref[at, :] - mm(lb_ref[at, :], y)).astype(BF)

        row_loop(tile)
        for s in range(4):
            at = pl.ds(s * ovl, ovl)
            face = mm(bf_ref[at, :], y) + mm(si_ref[at, :], wb[...])
            face_ref[at, :] = face + olds[s][...].astype(F32) if olds else face

    def local(y, base, olds):
        (face,) = call(
            k_local, [((nf, nrhs), F32)], y, base, lbmat, simat, bfac, *olds,
            scratch=[pltpu.VMEM((nloc, nrhs), BF)], name="local", flops=2 * nf * nloc * nrhs,
        )
        return face

    def k_faces(base_ref, f_ref, *refs):
        recvs, faces = refs[:4], refs[4:]
        recv = jnp.concatenate([x[...] for x in recvs], axis=0)
        for s, ref in enumerate(faces):
            at = pl.ds(s * ovl, ovl)
            ref[...] = (base_ref[at, :] + mm(f_ref[at, :], recv)).astype(BF)

    def faces_after(base, recv):
        return call(k_faces, [((ovl, nrhs), BF)] * 4, base, fmat, *recv, name="faces", flops=2 * nf * nf * nrhs)

    def k_advance(first, last, *refs):
        y_ref, base_ref, lb_ref, bt_ref, wt_ref, inv_ref, mat_ref, rhs_ref, basis_ref = refs[:9]
        recvs, refs = refs[9:13], refs[13:]
        old_ref, refs = (None, refs) if first else (refs[0], refs[1:])
        out_ref, res_ref = refs[:2]
        if last:
            wb, vb, recv, new_ref, sem = refs[2:]
        else:
            restr_ref, wb, vb, recv = refs[2:]
            new_ref = out_ref
        y = y_ref[...]
        for s, x in enumerate(recvs):
            recv[pl.ds(s * ovl, ovl), :] = x[...]

        def base_tile(at):
            wb[at, :] = (base_ref[at, :] - mm(lb_ref[at, :], y) + mm(wt_ref[at, :], recv[...])).astype(BF)

        row_loop(base_tile)

        def sol_tile(at):
            new = mm(bt_ref[at, :], y) + mm(inv_ref[at, :], wb[...])
            if not first:
                new = new + old_ref[at, :]
            new_ref[at, :] = new
            vb[at, :] = new.astype(BF)

        row_loop(sol_tile)
        if last:
            store = pltpu.make_async_copy(new_ref, out_ref, sem)
            store.start()

        def res_tile(at):
            res_ref[at, :] = rhs_ref[at, :] - mm(mat_ref[at, :], vb[...])

        row_loop(res_tile)
        if last:
            store.wait()
        else:
            restr_ref[...] = mm(basis_ref[...], res_ref[...].astype(BF))

    def advance(y, base, recv, old, last):
        first = old is None
        outs = [((nloc, nrhs), F32)] * 2 + ([] if last else [((cpd, nrhs), F32)])
        extra = [pltpu.VMEM((nloc, nrhs), F32), pltpu.SemaphoreType.DMA] if last else []
        return call(
            functools.partial(k_advance, first, last), outs,
            y, base, lbmat, btmat, wt, local_inv, local_mat, rhs, basis_t, *recv, *([] if first else [old]),
            scratch=[pltpu.VMEM((nloc, nrhs), BF)] * 2 + [pltpu.VMEM((nf, nrhs), BF)] + extra,
            hbm_outs=1 if last else 0, name="advance", flops=5 * nloc * nloc * nrhs,
        )

    def k_restrict_recv(base_ref, t_ref, *refs):
        recvs, out_ref = refs[:4], refs[4]
        recv = jnp.concatenate([x[...] for x in recvs], axis=0)
        out_ref[...] = (base_ref[...] + mm(t_ref[...], recv)).astype(BF)

    def k_couple(res_ref, wt_ref, *refs):
        recvs, out_ref, recv = refs[:4], refs[4], refs[5]
        for s, x in enumerate(recvs):
            recv[pl.ds(s * ovl, ovl), :] = x[...]

        def tile(at):
            out_ref[at, :] = res_ref[at, :] + mm(wt_ref[at, :], recv[...])

        row_loop(tile)

    def k_couple_last(res_ref, wt_ref, *refs):
        recvs, (out_ref, recv, buf, sems) = refs[:4], refs[4:]
        for s, x in enumerate(recvs):
            recv[pl.ds(s * ovl, ovl), :] = x[...]
        copies = []
        for i in range(nloc // last_step):
            at = pl.ds(i * last_step, last_step)
            buf[at, :] = res_ref[at, :] + mm(wt_ref[at, :], recv[...])
            copies.append(pltpu.make_async_copy(buf.at[at, :], out_ref.at[at, :], sems.at[i]))
            copies[-1].start()
        for copy in copies:
            copy.wait()

    def coupled(res, recv, last):
        extra = [pltpu.VMEM((nloc, nrhs), F32), pltpu.SemaphoreType.DMA((nloc // last_step,))] if last else []
        return call(
            k_couple_last if last else k_couple, [((nloc, nrhs), F32)], res, wt, *recv,
            scratch=[pltpu.VMEM((nf, nrhs), BF)] + extra, hbm_outs=1 if last else 0,
            name="couple", flops=2 * nloc * nf * nrhs,
        )[0]

    restricted = mm(basis_t, rhs.astype(BF)).astype(BF)
    table = jnp.concatenate([margin_rows[0].astype(F32), couple[0]], axis=0)
    sel, wt, inv_here = call(
        k_select, [((nf, nloc), BF), ((nloc, nf), BF), (coarse_inv.shape, BF)],
        coarse_inv, table, restricted, hbm_ins=1, tokens=1, name="select",
        scratch=[pltpu.SemaphoreType.DMA],
    )
    keep, recv = coarse_send(restricted, inv_here)
    bfac, tmat, simat, fmat, btmat, lbmat = call(
        k_products,
        [((nf, cpd), BF), ((cpd, nf), BF), ((nf, nloc), BF), ((nf, nf), BF), ((nloc, cpd), BF), ((nloc, cpd), BF)],
        sel, wt, local_inv, local_mat, basis_t, keep, tokens=1,
        name="products", flops=2 * nf * nloc * (nloc + nf + 3 * cpd),
    )
    token = tmat
    residual, solution, sent = rhs, None, []
    for sweep in range(STEPS):
        y, faces = coarse_faces(coarse_recv(keep, recv, token))
        recv = halo(faces)
        sent = faces_after(local(y, residual, sent), recv)
        recv2 = halo(sent)
        last = sweep == STEPS - 1
        new = advance(y, residual, recv, solution, last)
        solution, res = new[:2]
        if not last:
            (restricted,) = call(
                k_restrict_recv, [((cpd, nrhs), BF)], new[2], tmat, *recv2, name="restrict_recv",
            )
            keep, recv = coarse_send(restricted, inv_here)
        residual = coupled(res, recv2, last)
        token = residual
    return (solution, residual)


def solution(mesh):
    nr, nc = mesh.shape["row"], mesh.shape["col"]
    placed = (
        P(("row", "col"), None),
        P(("row", "col"), None),
        P(("row", "col"), None),
        P(("row", "col"), None),
        P("col", "row"),
        P(("row", "col"), None, None),
        P(("row", "col"), None, None),
    )
    return jax.shard_map(
        functools.partial(per_device, nr, nc),
        mesh=mesh,
        in_specs=placed,
        out_specs=(P(("row", "col"), None), P(("row", "col"), None)),
        check_vma=False,
    )
```

```python
import functools

import jax
import jax.numpy as jnp
from jax import lax
from jax.experimental import pallas as pl
from jax.experimental.pallas import tpu as pltpu
from jax.sharding import PartitionSpec as P

STEPS = 2
BF = jnp.bfloat16
F32 = jnp.float32
VMEM = pl.BlockSpec(memory_space=pltpu.VMEM)
ANY = pl.BlockSpec(memory_space=pl.ANY)
LIMIT = 24 << 20


def mm(a, b):
    return jnp.dot(a, b, preferred_element_type=F32)


def call(kernel, outs, *args, name, scratch=(), flops=0, hbm_ins=0, hbm_outs=0, tokens=0):
    nbytes = sum(a.size * a.dtype.itemsize for a in args)
    inner = len(args) - hbm_ins - tokens
    return pl.pallas_call(
        kernel,
        out_shape=[jax.ShapeDtypeStruct(s, d) for s, d in outs],
        in_specs=[ANY] * hbm_ins + [VMEM] * inner + [ANY] * tokens,
        out_specs=[ANY] * hbm_outs + [VMEM] * (len(outs) - hbm_outs),
        scratch_shapes=list(scratch),
        compiler_params=pltpu.CompilerParams(vmem_limit_bytes=LIMIT),
        cost_estimate=pl.CostEstimate(flops=flops, bytes_accessed=nbytes, transcendentals=0),
        name=name,
    )(*args)


def tiles(rows, most=512):
    return most if rows % most == 0 else rows


def per_device(nr, nc, rhs, local_mat, local_inv, basis_t, coarse_inv, couple, margin_rows):
    nloc, nrhs = rhs.shape
    cpd = basis_t.shape[0]
    ovl = margin_rows.shape[2]
    nf = 4 * ovl
    nz = nr // 2
    both = ("row", "col")

    step, last_step = tiles(nloc), tiles(nloc, 256)

    def row_loop(body):
        @pl.loop(0, nloc // step)
        def _(i):
            body(pl.ds(pl.multiple_of(i * step, step), step))

    def pairs(row_parity, col_parity):
        perm = {}
        for r in range(nr):
            for c in range(nc):
                if row_parity is not None:
                    o = r + 1 if r % 2 == row_parity else r - 1
                    other = (o, c) if 0 <= o < nr else (r, c ^ 1)
                else:
                    o = c + 1 if c % 2 == col_parity else c - 1
                    other = (r, o) if 0 <= o < nc else (r, nc - 1 - c)
                perm[r * nc + c] = other[0] * nc + other[1]
        return sorted(perm.items())

    slot_perms = [pairs(1, None), pairs(None, 1), pairs(0, None), pairs(None, 0)]

    def slot_faces():
        r, c = lax.axis_index("row"), lax.axis_index("col")
        pr, pc = lax.rem(r, 2), lax.rem(c, 2)
        one = lambda ok: jnp.where(ok, 1.0, 0.0).astype(F32)
        return [
            (pr, one((pr == 1) & (r + 1 < nr) | (pr == 0) & (r > 0))),
            (2 + pc, one((pc == 1) & (c + 1 < nc) | (pc == 0) & (c > 0))),
            (1 - pr, one((pr == 1) | (r + 1 < nr))),
            (3 - pc, one((pc == 1) | (c + 1 < nc))),
        ]

    def halo(faces):
        return [lax.ppermute(f, both, p) for f, p in zip(faces, slot_perms)]

    def k_select(table_ref, token, sel_ref, wt_ref):
        for s, (k, ok) in enumerate(slot_faces()):
            row = table_ref[pl.ds(k, 1), :].astype(jnp.int32)
            w = table_ref[pl.ds(4 + k, 1), :] * ok
            at = pl.ds(s * ovl, ovl)
            down = lax.broadcasted_iota(jnp.int32, (nloc, ovl), 0)
            wt_ref[:, at] = jnp.where(down == row, jnp.broadcast_to(w, (nloc, ovl)), 0.0).astype(BF)
            idx = jnp.broadcast_to(row.astype(F32), (ovl, ovl)).T
            for j in range(nloc // ovl):
                across = lax.broadcasted_iota(jnp.int32, (ovl, ovl), 1) + j * ovl
                sel_ref[at, pl.ds(j * ovl, ovl)] = jnp.where(idx == across.astype(F32), 1.0, 0.0).astype(BF)

    def k_products(sel_ref, wt_ref, inv_ref, basis_ref, bf_ref, t_ref, si_ref, f_ref, bt_ref):
        bt = basis_ref[...].astype(F32).T.astype(BF)
        bt_ref[...] = bt
        bf_ref[...] = mm(sel_ref[...], bt).astype(BF)
        t_ref[...] = mm(basis_ref[...], wt_ref[...]).astype(BF)
        fstep = tiles(nf)

        @pl.loop(0, nf // fstep)
        def _(i):
            at = pl.ds(pl.multiple_of(i * fstep, fstep), fstep)
            si_ref[at, :] = mm(sel_ref[at, :], inv_ref[...]).astype(BF)
            f_ref[at, :] = mm(si_ref[at, :], wt_ref[...]).astype(BF)

    def k_mat_basis(mat_ref, bt_ref, token, lb_ref):
        def tile(at):
            lb_ref[at, :] = mm(mat_ref[at, :], bt_ref[...]).astype(BF)

        row_loop(tile)

    half = nz * cpd

    def k_hold(inv_ref, token, same_ref, cross_ref):
        r = lax.axis_index("row")
        for i in range(nz):
            at = pl.ds(i * cpd, cpd)
            same_ref[at, :] = inv_ref[pl.ds(pl.multiple_of((r ^ (2 * i)) * cpd, 16), cpd), :]
            cross_ref[at, :] = inv_ref[pl.ds(pl.multiple_of((r ^ (2 * i + 1)) * cpd, 16), cpd), :]

    def place(group, blocks):
        c = lax.axis_index("col")
        for i, block in enumerate(blocks):
            group[pl.ds(pl.multiple_of((c ^ i) * cpd, 16), cpd), :] = block[...]

    def k_coarse(*refs):
        blocks, (same_ref, cross_ref, keep_ref, send_ref, group) = refs[:nc], refs[nc:]
        place(group, blocks)
        send_ref[...] = mm(cross_ref[...], group[...]).astype(BF)
        keep_ref[...] = mm(same_ref[...], group[...])

    def k_half(keep_ref, recv_ref, token, own_ref, *sends):
        own_ref[...] = keep_ref[pl.ds(0, cpd), :] + recv_ref[pl.ds(0, cpd), :].astype(F32)
        for i, ref in enumerate(sends):
            at = pl.ds((i + 1) * cpd, cpd)
            ref[...] = (keep_ref[at, :] + recv_ref[at, :].astype(F32)).astype(BF)

    def k_coarse_pair(*refs):
        mine, theirs, refs = refs[:nc], refs[nc : 2 * nc], refs[2 * nc :]
        same_ref, other_ref, token, own_ref = refs[:4]
        sends, (group, group_other) = refs[4:-2], refs[-2:]
        place(group, mine)
        place(group_other, theirs)
        for i, ref in enumerate((own_ref,) + tuple(sends)):
            at = pl.ds(i * cpd, cpd)
            ref[...] = (mm(same_ref[at, :], group[...]) + mm(other_ref[at, :], group_other[...])).astype(ref.dtype)

    def over_col(block):
        return [block] + [
            lax.ppermute(block, "col", [(i, i ^ k) for i in range(nc)]) for k in reversed(range(1, nc))
        ][::-1]

    def over_pair(value):
        return lax.ppermute(value, "row", [(i, i ^ 1) for i in range(nr)])

    def reduce_rows(own, sends):
        return [own] + [
            lax.ppermute(s, "row", [(i, i ^ (2 * (k + 1))) for i in range(nr)]) for k, s in enumerate(sends)
        ]

    own_and_sends = [((cpd, nrhs), F32)] + [((cpd, nrhs), BF)] * (nz - 1)

    def k_coarse_faces(*refs):
        parts, (bf_ref, y_ref), faces = refs[:nz], refs[nz : nz + 2], refs[nz + 2 :]
        total = parts[0][...]
        for p in parts[1:]:
            total = total + p[...].astype(F32)
        y = total.astype(BF)
        y_ref[...] = y
        for s, ref in enumerate(faces):
            ref[...] = mm(bf_ref[pl.ds(s * ovl, ovl), :], y).astype(BF)

    def coarse_faces(parts):
        y, *faces = call(
            k_coarse_faces, [((cpd, nrhs), BF)] + [((ovl, nrhs), BF)] * 4, *parts, bfac, name="coarse_faces",
        )
        return y, faces

    def k_local(y_ref, base_ref, lb_ref, si_ref, bf_ref, *refs):
        olds, face_ref, wb = refs[:-2], refs[-2], refs[-1]
        y = y_ref[...]

        def tile(at):
            wb[at, :] = (base_ref[at, :] - mm(lb_ref[at, :], y)).astype(BF)

        row_loop(tile)
        for s in range(4):
            at = pl.ds(s * ovl, ovl)
            face = mm(bf_ref[at, :], y) + mm(si_ref[at, :], wb[...])
            face_ref[at, :] = face + olds[s][...].astype(F32) if olds else face

    def local(y, base, olds):
        (face,) = call(
            k_local, [((nf, nrhs), F32)], y, base, lbmat, simat, bfac, *olds,
            scratch=[pltpu.VMEM((nloc, nrhs), BF)], name="local", flops=2 * nf * nloc * nrhs,
        )
        return face

    def k_faces(base_ref, f_ref, *refs):
        recvs, faces = refs[:4], refs[4:]
        recv = jnp.concatenate([x[...] for x in recvs], axis=0)
        for s, ref in enumerate(faces):
            at = pl.ds(s * ovl, ovl)
            ref[...] = (base_ref[at, :] + mm(f_ref[at, :], recv)).astype(BF)

    def faces_after(base, recv):
        return call(k_faces, [((ovl, nrhs), BF)] * 4, base, fmat, *recv, name="faces", flops=2 * nf * nf * nrhs)

    def k_advance(first, last, *refs):
        y_ref, base_ref, lb_ref, bt_ref, wt_ref, inv_ref, mat_ref, rhs_ref, basis_ref = refs[:9]
        recvs, refs = refs[9:13], refs[13:]
        old_ref, refs = (None, refs) if first else (refs[0], refs[1:])
        out_ref, res_ref = refs[:2]
        if last:
            wb, vb, recv, new_ref, sem = refs[2:]
        else:
            restr_ref, wb, vb, recv = refs[2:]
            new_ref = out_ref
        y = y_ref[...]
        for s, x in enumerate(recvs):
            recv[pl.ds(s * ovl, ovl), :] = x[...]

        def base_tile(at):
            wb[at, :] = (base_ref[at, :] - mm(lb_ref[at, :], y) + mm(wt_ref[at, :], recv[...])).astype(BF)

        row_loop(base_tile)

        def sol_tile(at):
            new = mm(bt_ref[at, :], y) + mm(inv_ref[at, :], wb[...])
            if not first:
                new = new + old_ref[at, :]
            new_ref[at, :] = new
            vb[at, :] = new.astype(BF)

        row_loop(sol_tile)
        if last:
            store = pltpu.make_async_copy(new_ref, out_ref, sem)
            store.start()

        def res_tile(at):
            res_ref[at, :] = rhs_ref[at, :] - mm(mat_ref[at, :], vb[...])

        row_loop(res_tile)
        if last:
            store.wait()
        else:
            restr_ref[...] = mm(basis_ref[...], res_ref[...].astype(BF))

    def advance(y, base, recv, old, last):
        first = old is None
        outs = [((nloc, nrhs), F32)] * 2 + ([] if last else [((cpd, nrhs), F32)])
        extra = [pltpu.VMEM((nloc, nrhs), F32), pltpu.SemaphoreType.DMA] if last else []
        return call(
            functools.partial(k_advance, first, last), outs,
            y, base, lbmat, btmat, wt, local_inv, local_mat, rhs, basis_t, *recv, *([] if first else [old]),
            scratch=[pltpu.VMEM((nloc, nrhs), BF)] * 2 + [pltpu.VMEM((nf, nrhs), BF)] + extra,
            hbm_outs=1 if last else 0, name="advance", flops=5 * nloc * nloc * nrhs,
        )

    def k_restrict_recv(base_ref, t_ref, *refs):
        recvs, out_ref = refs[:4], refs[4]
        recv = jnp.concatenate([x[...] for x in recvs], axis=0)
        out_ref[...] = (base_ref[...] + mm(t_ref[...], recv)).astype(BF)

    def k_couple(res_ref, wt_ref, *refs):
        recvs, out_ref, recv = refs[:4], refs[4], refs[5]
        for s, x in enumerate(recvs):
            recv[pl.ds(s * ovl, ovl), :] = x[...]

        def tile(at):
            out_ref[at, :] = res_ref[at, :] + mm(wt_ref[at, :], recv[...])

        row_loop(tile)

    def k_couple_last(res_ref, wt_ref, *refs):
        recvs, (out_ref, recv, buf, sems) = refs[:4], refs[4:]
        for s, x in enumerate(recvs):
            recv[pl.ds(s * ovl, ovl), :] = x[...]
        copies = []
        for i in range(nloc // last_step):
            at = pl.ds(i * last_step, last_step)
            buf[at, :] = res_ref[at, :] + mm(wt_ref[at, :], recv[...])
            copies.append(pltpu.make_async_copy(buf.at[at, :], out_ref.at[at, :], sems.at[i]))
            copies[-1].start()
        for copy in copies:
            copy.wait()

    def coupled(res, recv, last):
        extra = [pltpu.VMEM((nloc, nrhs), F32), pltpu.SemaphoreType.DMA((nloc // last_step,))] if last else []
        return call(
            k_couple_last if last else k_couple, [((nloc, nrhs), F32)], res, wt, *recv,
            scratch=[pltpu.VMEM((nf, nrhs), BF)] + extra, hbm_outs=1 if last else 0,
            name="couple", flops=2 * nloc * nf * nrhs,
        )[0]

    restricted = mm(basis_t, rhs.astype(BF)).astype(BF)
    blocks = over_col(restricted)
    same, cross = call(
        k_hold, [((half, coarse_inv.shape[1]), BF)] * 2, coarse_inv, restricted, tokens=1, name="hold",
    )
    keep, send = call(
        k_coarse, [((half, nrhs), F32), ((half, nrhs), BF)], *blocks, same, cross,
        scratch=[pltpu.VMEM((nc * cpd, nrhs), BF)], name="coarse", flops=4 * half * nc * cpd * nrhs,
    )
    arrived = over_pair(send)
    other = over_pair(cross)
    table = jnp.concatenate([margin_rows[0].astype(F32), couple[0]], axis=0)
    sel, wt = call(k_select, [((nf, nloc), BF), ((nloc, nf), BF)], table, keep, tokens=1, name="select")
    bfac, tmat, simat, fmat, btmat = call(
        k_products,
        [((nf, cpd), BF), ((cpd, nf), BF), ((nf, nloc), BF), ((nf, nf), BF), ((nloc, cpd), BF)],
        sel, wt, local_inv, basis_t, name="products", flops=2 * nf * nloc * (nloc + nf + 2 * cpd),
    )
    own, *sends = call(k_half, own_and_sends, keep, arrived, tmat, tokens=1, name="half")
    (lbmat,) = call(
        k_mat_basis, [((nloc, cpd), BF)], local_mat, btmat, own, tokens=1,
        name="mat_basis", flops=2 * nloc * nloc * cpd,
    )
    residual, solution, sent = rhs, None, []
    for sweep in range(STEPS):
        y, faces = coarse_faces(reduce_rows(own, sends))
        recv = halo(faces)
        sent = faces_after(local(y, residual, sent), recv)
        recv2 = halo(sent)
        last = sweep == STEPS - 1
        new = advance(y, residual, recv, solution, last)
        solution, res = new[:2]
        residual = coupled(res, recv2, last)
        if not last:
            (restricted,) = call(
                k_restrict_recv, [((cpd, nrhs), BF)], new[2], tmat, *recv2, name="restrict_recv",
            )
            across = over_pair(restricted)
            own, *sends = call(
                k_coarse_pair, own_and_sends, *over_col(restricted), *over_col(across), same, other, residual,
                scratch=[pltpu.VMEM((nc * cpd, nrhs), BF)] * 2, tokens=1,
                name="coarse_pair", flops=4 * half * nc * cpd * nrhs,
            )
    return (solution, residual)


def solution(mesh):
    nr, nc = mesh.shape["row"], mesh.shape["col"]
    placed = (
        P(("row", "col"), None),
        P(("row", "col"), None),
        P(("row", "col"), None),
        P(("row", "col"), None),
        P("col", "row"),
        P(("row", "col"), None, None),
        P(("row", "col"), None, None),
    )
    return jax.shard_map(
        functools.partial(per_device, nr, nc),
        mesh=mesh,
        in_specs=placed,
        out_specs=(P(("row", "col"), None), P(("row", "col"), None)),
        check_vma=False,
    )
```

```python
import functools

import jax
import jax.numpy as jnp
from jax import lax
from jax.experimental import pallas as pl
from jax.experimental.pallas import tpu as pltpu
from jax.sharding import PartitionSpec as P


STEPS = 2
BF = jnp.bfloat16
F32 = jnp.float32
VMEM = pl.BlockSpec(memory_space=pltpu.VMEM)
ANY = pl.BlockSpec(memory_space=pl.ANY)
LIMIT = 24 << 20


def mm(a, b):
    return jnp.dot(a, b, preferred_element_type=F32)


def call(kernel, outs, *args, scratch=(), flops=0, hbm_ins=0, hbm_outs=0, tokens=0):
    nbytes = sum(a.size * a.dtype.itemsize for a in args)
    inner = len(args) - hbm_ins - tokens
    return pl.pallas_call(
        kernel,
        out_shape=[jax.ShapeDtypeStruct(s, d) for s, d in outs],
        in_specs=[ANY] * hbm_ins + [VMEM] * inner + [ANY] * tokens,
        out_specs=[ANY] * hbm_outs + [VMEM] * (len(outs) - hbm_outs),
        scratch_shapes=list(scratch),
        compiler_params=pltpu.CompilerParams(vmem_limit_bytes=LIMIT),
        cost_estimate=pl.CostEstimate(flops=flops, bytes_accessed=nbytes, transcendentals=0),
    )(*args)


def tiles(rows, most=512):
    return most if rows % most == 0 else rows


def per_device(nr, nc, rhs, local_mat, local_inv, basis_t, coarse_inv, couple, margin_rows):
    nloc, nrhs = rhs.shape
    cpd = basis_t.shape[0]
    ovl = margin_rows.shape[2]
    nf = 4 * ovl
    nz = nr // 2
    both = ("row", "col")

    step, last_step = tiles(nloc), tiles(nloc, 256)

    def row_loop(body):
        @pl.loop(0, nloc // step)
        def _(i):
            body(pl.ds(pl.multiple_of(i * step, step), step))

    def pairs(row_parity, col_parity):
        perm = {}
        for r in range(nr):
            for c in range(nc):
                if row_parity is not None:
                    o = r + 1 if r % 2 == row_parity else r - 1
                    other = (o, c) if 0 <= o < nr else (r, c ^ 1)
                else:
                    o = c + 1 if c % 2 == col_parity else c - 1
                    other = (r, o) if 0 <= o < nc else (r, nc - 1 - c)
                perm[r * nc + c] = other[0] * nc + other[1]
        return sorted(perm.items())

    slot_perms = [pairs(1, None), pairs(None, 1), pairs(0, None), pairs(None, 0)]

    def slot_faces():
        r, c = lax.axis_index("row"), lax.axis_index("col")
        pr, pc = lax.rem(r, 2), lax.rem(c, 2)
        one = lambda ok: jnp.where(ok, 1.0, 0.0).astype(F32)
        return [
            (pr, one((pr == 1) & (r + 1 < nr) | (pr == 0) & (r > 0))),
            (2 + pc, one((pc == 1) & (c + 1 < nc) | (pc == 0) & (c > 0))),
            (1 - pr, one((pr == 1) | (r + 1 < nr))),
            (3 - pc, one((pc == 1) | (c + 1 < nc))),
        ]

    def halo(faces):
        return [lax.ppermute(f, both, p) for f, p in zip(faces, slot_perms)]

    def k_select(table_ref, token, sel_ref, wt_ref):
        for s, (k, ok) in enumerate(slot_faces()):
            row = table_ref[pl.ds(k, 1), :].astype(jnp.int32)
            w = table_ref[pl.ds(4 + k, 1), :] * ok
            at = pl.ds(s * ovl, ovl)
            down = lax.broadcasted_iota(jnp.int32, (nloc, ovl), 0)
            wt_ref[:, at] = jnp.where(down == row, jnp.broadcast_to(w, (nloc, ovl)), 0.0).astype(BF)
            idx = jnp.broadcast_to(row.astype(F32), (ovl, ovl)).T
            for j in range(nloc // ovl):
                across = lax.broadcasted_iota(jnp.int32, (ovl, ovl), 1) + j * ovl
                sel_ref[at, pl.ds(j * ovl, ovl)] = jnp.where(idx == across.astype(F32), 1.0, 0.0).astype(BF)

    def k_products(sel_ref, wt_ref, inv_ref, basis_ref, token, bf_ref, t_ref, si_ref, f_ref, bt_ref):
        bt = basis_ref[...].astype(F32).T.astype(BF)
        bt_ref[...] = bt
        bf_ref[...] = mm(sel_ref[...], bt).astype(BF)
        t_ref[...] = mm(basis_ref[...], wt_ref[...]).astype(BF)
        fstep = tiles(nf)

        @pl.loop(0, nf // fstep)
        def _(i):
            at = pl.ds(pl.multiple_of(i * fstep, fstep), fstep)
            si_ref[at, :] = mm(sel_ref[at, :], inv_ref[...]).astype(BF)
            f_ref[at, :] = mm(si_ref[at, :], wt_ref[...]).astype(BF)

    def k_mat_basis(mat_ref, bt_ref, token, lb_ref):
        def tile(at):
            lb_ref[at, :] = mm(mat_ref[at, :], bt_ref[...]).astype(BF)

        row_loop(tile)

    half = nz * cpd

    def k_lead(out_ref):
        out_ref[...] = jnp.zeros_like(out_ref)

    def k_hold(inv_ref, block_ref, token, same_ref, cross_ref, out_ref):
        r = lax.axis_index("row")
        out_ref[...] = block_ref[...]
        for i in range(nz):
            at = pl.ds(i * cpd, cpd)
            same_ref[at, :] = inv_ref[pl.ds(pl.multiple_of((r ^ (2 * i)) * cpd, 16), cpd), :]
            cross_ref[at, :] = inv_ref[pl.ds(pl.multiple_of((r ^ (2 * i + 1)) * cpd, 16), cpd), :]

    def place(group, blocks):
        c = lax.axis_index("col")
        for i, block in enumerate(blocks):
            group[pl.ds(pl.multiple_of((c ^ i) * cpd, 16), cpd), :] = block[...]

    def k_coarse_pair(*refs):
        mine, theirs, refs = refs[:nc], refs[nc : 2 * nc], refs[2 * nc :]
        same_ref, other_ref, _, own_ref = refs[:4]
        sends, (group, group_other) = refs[4:-2], refs[-2:]
        place(group, mine)
        place(group_other, theirs)
        for i, ref in enumerate((own_ref,) + tuple(sends)):
            at = pl.ds(i * cpd, cpd)
            ref[...] = (mm(same_ref[at, :], group[...]) + mm(other_ref[at, :], group_other[...])).astype(ref.dtype)

    def over_col(block):
        return [block] + [
            lax.ppermute(block, "col", [(i, i ^ k) for i in range(nc)]) for k in reversed(range(1, nc))
        ][::-1]

    def over_pair(value):
        return lax.ppermute(value, "row", [(i, i ^ 1) for i in range(nr)])

    def reduce_rows(own, sends):
        return [own] + [
            lax.ppermute(s, "row", [(i, i ^ (2 * (k + 1))) for i in range(nr)]) for k, s in enumerate(sends)
        ]

    own_and_sends = [((cpd, nrhs), F32)] + [((cpd, nrhs), BF)] * (nz - 1)

    def k_coarse_faces(*refs):
        parts, (bf_ref, y_ref), faces = refs[:nz], refs[nz : nz + 2], refs[nz + 2 :]
        total = parts[0][...]
        for p in parts[1:]:
            total = total + p[...].astype(F32)
        y = total.astype(BF)
        y_ref[...] = y
        for s, ref in enumerate(faces):
            ref[...] = mm(bf_ref[pl.ds(s * ovl, ovl), :], y).astype(BF)

    def coarse_faces(parts):
        y, *faces = call(k_coarse_faces, [((cpd, nrhs), BF)] + [((ovl, nrhs), BF)] * 4, *parts, bfac)
        return y, faces

    def k_local(y_ref, base_ref, lb_ref, si_ref, bf_ref, *refs):
        olds, face_ref, wb = refs[:-2], refs[-2], refs[-1]
        y = y_ref[...]

        def tile(at):
            wb[at, :] = (base_ref[at, :] - mm(lb_ref[at, :], y)).astype(BF)

        row_loop(tile)
        for s in range(4):
            at = pl.ds(s * ovl, ovl)
            face = mm(bf_ref[at, :], y) + mm(si_ref[at, :], wb[...])
            face_ref[at, :] = face + olds[s][...].astype(F32) if olds else face

    def local(y, base, olds):
        (face,) = call(
            k_local, [((nf, nrhs), F32)], y, base, lbmat, simat, bfac, *olds,
            scratch=[pltpu.VMEM((nloc, nrhs), BF)], flops=2 * nf * nloc * nrhs,
        )
        return face

    def k_faces(base_ref, f_ref, *refs):
        recvs, faces = refs[:4], refs[4:]
        recv = jnp.concatenate([x[...] for x in recvs], axis=0)
        for s, ref in enumerate(faces):
            at = pl.ds(s * ovl, ovl)
            ref[...] = (base_ref[at, :] + mm(f_ref[at, :], recv)).astype(BF)

    def faces_after(base, recv):
        return call(k_faces, [((ovl, nrhs), BF)] * 4, base, fmat, *recv, flops=2 * nf * nf * nrhs)

    def k_advance(first, last, *refs):
        y_ref, base_ref, lb_ref, bt_ref, wt_ref, inv_ref, mat_ref, rhs_ref, basis_ref = refs[:9]
        recvs, refs = refs[9:13], refs[13:]
        old_ref, refs = (None, refs) if first else (refs[0], refs[1:])
        out_ref, res_ref = refs[:2]
        if last:
            wb, vb, recv, new_ref, sem = refs[2:]
        else:
            restr_ref, wb, vb, recv = refs[2:]
            new_ref = out_ref
        y = y_ref[...]
        for s, x in enumerate(recvs):
            recv[pl.ds(s * ovl, ovl), :] = x[...]

        def base_tile(at):
            wb[at, :] = (base_ref[at, :] - mm(lb_ref[at, :], y) + mm(wt_ref[at, :], recv[...])).astype(BF)

        row_loop(base_tile)

        def sol_tile(at):
            new = mm(bt_ref[at, :], y) + mm(inv_ref[at, :], wb[...])
            if not first:
                new = new + old_ref[at, :]
            new_ref[at, :] = new
            vb[at, :] = new.astype(BF)

        row_loop(sol_tile)
        if last:
            store = pltpu.make_async_copy(new_ref, out_ref, sem)
            store.start()

        def res_tile(at):
            res_ref[at, :] = rhs_ref[at, :] - mm(mat_ref[at, :], vb[...])

        row_loop(res_tile)
        if last:
            store.wait()
        else:
            restr_ref[...] = mm(basis_ref[...], res_ref[...].astype(BF))

    def advance(y, base, recv, old, last):
        first = old is None
        outs = [((nloc, nrhs), F32)] * 2 + ([] if last else [((cpd, nrhs), F32)])
        extra = [pltpu.VMEM((nloc, nrhs), F32), pltpu.SemaphoreType.DMA] if last else []
        return call(
            functools.partial(k_advance, first, last), outs,
            y, base, lbmat, btmat, wt, local_inv, local_mat, rhs, basis_t, *recv, *([] if first else [old]),
            scratch=[pltpu.VMEM((nloc, nrhs), BF)] * 2 + [pltpu.VMEM((nf, nrhs), BF)] + extra,
            hbm_outs=1 if last else 0, flops=5 * nloc * nloc * nrhs,
        )

    def k_restrict_recv(base_ref, t_ref, *refs):
        recvs, out_ref = refs[:4], refs[4]
        recv = jnp.concatenate([x[...] for x in recvs], axis=0)
        out_ref[...] = (base_ref[...] + mm(t_ref[...], recv)).astype(BF)

    def k_couple(res_ref, wt_ref, *refs):
        recvs, out_ref, recv = refs[:4], refs[4], refs[5]
        for s, x in enumerate(recvs):
            recv[pl.ds(s * ovl, ovl), :] = x[...]

        def tile(at):
            out_ref[at, :] = res_ref[at, :] + mm(wt_ref[at, :], recv[...])

        row_loop(tile)

    def k_couple_last(res_ref, wt_ref, *refs):
        recvs, (out_ref, recv, buf, sems) = refs[:4], refs[4:]
        for s, x in enumerate(recvs):
            recv[pl.ds(s * ovl, ovl), :] = x[...]
        copies = []
        for i in range(nloc // last_step):
            at = pl.ds(i * last_step, last_step)
            buf[at, :] = res_ref[at, :] + mm(wt_ref[at, :], recv[...])
            copies.append(pltpu.make_async_copy(buf.at[at, :], out_ref.at[at, :], sems.at[i]))
            copies[-1].start()
        for copy in copies:
            copy.wait()

    def coupled(res, recv, last):
        extra = [pltpu.VMEM((nloc, nrhs), F32), pltpu.SemaphoreType.DMA((nloc // last_step,))] if last else []
        return call(
            k_couple_last if last else k_couple, [((nloc, nrhs), F32)], res, wt, *recv,
            scratch=[pltpu.VMEM((nf, nrhs), BF)] + extra, hbm_outs=1 if last else 0,
            flops=2 * nloc * nf * nrhs,
        )[0]

    def coarse_pair(mine, across, token):
        return call(
            k_coarse_pair, own_and_sends, *mine, *over_col(across), same, other, token,
            scratch=[pltpu.VMEM((nc * cpd, nrhs), BF)] * 2, tokens=1,
            flops=4 * half * nc * cpd * nrhs,
        )

    (lead,) = call(k_lead, [((8, 128), F32)], flops=8 * nloc * nloc * nrhs)
    restricted = mm(basis_t, rhs.astype(BF)).astype(BF)
    same, cross, restricted = call(
        k_hold, [((half, coarse_inv.shape[1]), BF)] * 2 + [((cpd, nrhs), BF)], coarse_inv, restricted, lead,
        tokens=1,
    )
    across = over_pair(restricted)
    other = over_pair(cross)
    mine = over_col(restricted)
    table = jnp.concatenate([margin_rows[0].astype(F32), couple[0]], axis=0)
    sel, wt = call(k_select, [((nf, nloc), BF), ((nloc, nf), BF)], table, restricted, tokens=1)
    own, *sends = coarse_pair(mine, across, wt)
    bfac, tmat, simat, fmat, btmat = call(
        k_products,
        [((nf, cpd), BF), ((cpd, nf), BF), ((nf, nloc), BF), ((nf, nf), BF), ((nloc, cpd), BF)],
        sel, wt, local_inv, basis_t, own, tokens=1, flops=2 * nf * nloc * (nloc + nf + 2 * cpd),
    )
    (lbmat,) = call(
        k_mat_basis, [((nloc, cpd), BF)], local_mat, btmat, own, tokens=1,
        flops=2 * nloc * nloc * cpd,
    )
    residual, solution, sent = rhs, None, []
    for sweep in range(STEPS):
        y, faces = coarse_faces(reduce_rows(own, sends))
        recv = halo(faces)
        sent = faces_after(local(y, residual, sent), recv)
        recv2 = halo(sent)
        last = sweep == STEPS - 1
        new = advance(y, residual, recv, solution, last)
        solution, res = new[:2]
        residual = coupled(res, recv2, last)
        if not last:
            (restricted,) = call(k_restrict_recv, [((cpd, nrhs), BF)], new[2], tmat, *recv2)
            own, *sends = coarse_pair(over_col(restricted), over_pair(restricted), residual)
    return (solution, residual)


def solution(mesh):
    nr, nc = mesh.shape["row"], mesh.shape["col"]
    placed = (
        P(("row", "col"), None),
        P(("row", "col"), None),
        P(("row", "col"), None),
        P(("row", "col"), None),
        P("col", "row"),
        P(("row", "col"), None, None),
        P(("row", "col"), None, None),
    )
    return jax.shard_map(
        functools.partial(per_device, nr, nc),
        mesh=mesh,
        in_specs=placed,
        out_specs=(P(("row", "col"), None), P(("row", "col"), None)),
        check_vma=False,
    )
```

```python
import functools

import jax
import jax.numpy as jnp
from jax import lax
from jax.experimental import pallas as pl
from jax.experimental.pallas import tpu as pltpu
from jax.sharding import PartitionSpec as P


STEPS = 2
BF = jnp.bfloat16
F32 = jnp.float32
VMEM = pl.BlockSpec(memory_space=pltpu.VMEM)
ANY = pl.BlockSpec(memory_space=pl.ANY)
LIMIT = 24 << 20


def mm(a, b):
    return jnp.dot(a, b, preferred_element_type=F32)


def call(kernel, outs, *args, scratch=(), flops=0, hbm_ins=0, hbm_outs=0, tokens=0):
    nbytes = sum(a.size * a.dtype.itemsize for a in args)
    inner = len(args) - hbm_ins - tokens
    return pl.pallas_call(
        kernel,
        out_shape=[jax.ShapeDtypeStruct(s, d) for s, d in outs],
        in_specs=[ANY] * hbm_ins + [VMEM] * inner + [ANY] * tokens,
        out_specs=[ANY] * hbm_outs + [VMEM] * (len(outs) - hbm_outs),
        scratch_shapes=list(scratch),
        compiler_params=pltpu.CompilerParams(vmem_limit_bytes=LIMIT),
        cost_estimate=pl.CostEstimate(flops=flops, bytes_accessed=nbytes, transcendentals=0),
    )(*args)


def tiles(rows, most=512):
    return most if rows % most == 0 else rows


def per_device(nr, nc, rhs, local_mat, local_inv, basis_t, coarse_inv, couple, margin_rows):
    nloc, nrhs = rhs.shape
    cpd = basis_t.shape[0]
    ovl = margin_rows.shape[2]
    nf = 4 * ovl
    nz = nr // 2
    both = ("row", "col")

    step, last_step = tiles(nloc), tiles(nloc, 256)

    def row_loop(body):
        @pl.loop(0, nloc // step)
        def _(i):
            body(pl.ds(pl.multiple_of(i * step, step), step))

    def pairs(row_parity, col_parity):
        perm = {}
        for r in range(nr):
            for c in range(nc):
                if row_parity is not None:
                    o = r + 1 if r % 2 == row_parity else r - 1
                    other = (o, c) if 0 <= o < nr else (r, c ^ 1)
                else:
                    o = c + 1 if c % 2 == col_parity else c - 1
                    other = (r, o) if 0 <= o < nc else (r, nc - 1 - c)
                perm[r * nc + c] = other[0] * nc + other[1]
        return sorted(perm.items())

    slot_perms = [pairs(1, None), pairs(None, 1), pairs(0, None), pairs(None, 0)]

    def slot_faces():
        r, c = lax.axis_index("row"), lax.axis_index("col")
        pr, pc = lax.rem(r, 2), lax.rem(c, 2)
        one = lambda ok: jnp.where(ok, 1.0, 0.0).astype(F32)
        return [
            (pr, one((pr == 1) & (r + 1 < nr) | (pr == 0) & (r > 0))),
            (2 + pc, one((pc == 1) & (c + 1 < nc) | (pc == 0) & (c > 0))),
            (1 - pr, one((pr == 1) | (r + 1 < nr))),
            (3 - pc, one((pc == 1) | (c + 1 < nc))),
        ]

    def halo(faces):
        out = []
        for f, p in zip(faces, slot_perms):
            out.append(lax.ppermute(f, both, p))
        return out

    def k_select(table_ref, basis_ref, token, sel_ref, wt_ref, bt_ref):
        bt_ref[...] = basis_ref[...].astype(F32).T.astype(BF)
        for s, (k, ok) in enumerate(slot_faces()):
            row = table_ref[pl.ds(k, 1), :].astype(jnp.int32)
            w = table_ref[pl.ds(4 + k, 1), :] * ok
            at = pl.ds(s * ovl, ovl)
            down = lax.broadcasted_iota(jnp.int32, (nloc, ovl), 0)
            wt_ref[:, at] = jnp.where(down == row, jnp.broadcast_to(w, (nloc, ovl)), 0.0).astype(BF)
            idx = jnp.broadcast_to(row.astype(F32), (ovl, ovl)).T
            for j in range(nloc // ovl):
                across = lax.broadcasted_iota(jnp.int32, (ovl, ovl), 1) + j * ovl
                sel_ref[at, pl.ds(j * ovl, ovl)] = jnp.where(idx == across.astype(F32), 1.0, 0.0).astype(BF)

    def k_products(sel_ref, wt_ref, inv_ref, bt_ref, token, bf_ref, si_ref, f_ref):
        bf_ref[...] = mm(sel_ref[...], bt_ref[...]).astype(BF)
        fstep = tiles(nf)

        @pl.loop(0, nf // fstep)
        def _(i):
            at = pl.ds(pl.multiple_of(i * fstep, fstep), fstep)
            si_ref[at, :] = mm(sel_ref[at, :], inv_ref[...]).astype(BF)
            f_ref[at, :] = mm(si_ref[at, :], wt_ref[...]).astype(BF)

    def k_mat_basis(mat_ref, bt_ref, token, lb_ref):
        def tile(at):
            lb_ref[at, :] = mm(mat_ref[at, :], bt_ref[...]).astype(BF)

        row_loop(tile)

    def k_restrictors(basis_ref, mat_ref, wt_ref, rhs_ref, token, z_ref, t_ref, brhs_ref):
        z_ref[...] = mm(basis_ref[...], mat_ref[...]).astype(BF)
        t_ref[...] = mm(basis_ref[...], wt_ref[...]).astype(BF)
        brhs_ref[...] = mm(basis_ref[...], rhs_ref[...].astype(BF))

    half = nz * cpd

    def k_lead(out_ref):
        out_ref[...] = jnp.zeros_like(out_ref)

    def k_hold(inv_ref, block_ref, token, same_ref, cross_ref, out_ref):
        r = lax.axis_index("row")
        out_ref[...] = block_ref[...]
        for i in range(nz):
            at = pl.ds(i * cpd, cpd)
            same_ref[at, :] = inv_ref[pl.ds(pl.multiple_of((r ^ (2 * i)) * cpd, 16), cpd), :]
            cross_ref[at, :] = inv_ref[pl.ds(pl.multiple_of((r ^ (2 * i + 1)) * cpd, 16), cpd), :]

    def place(group, blocks):
        c = lax.axis_index("col")
        for i, block in enumerate(blocks):
            group[pl.ds(pl.multiple_of((c ^ i) * cpd, 16), cpd), :] = block[...]

    def k_coarse_pair(*refs):
        mine, theirs, refs = refs[:nc], refs[nc : 2 * nc], refs[2 * nc :]
        same_ref, other_ref, _, own_ref = refs[:4]
        sends, (group, group_other) = refs[4:-2], refs[-2:]
        place(group, mine)
        place(group_other, theirs)
        for i, ref in enumerate((own_ref,) + tuple(sends)):
            at = pl.ds(i * cpd, cpd)
            ref[...] = (mm(same_ref[at, :], group[...]) + mm(other_ref[at, :], group_other[...])).astype(ref.dtype)

    def over_col(block):
        return [block] + [
            lax.ppermute(block, "col", [(i, i ^ k) for i in range(nc)]) for k in reversed(range(1, nc))
        ][::-1]

    def over_pair(value):
        return lax.ppermute(value, "row", [(i, i ^ 1) for i in range(nr)])

    def reduce_rows(own, sends):
        out = [own]
        for k, block in enumerate(sends):
            out.append(lax.ppermute(block, "row", [(i, i ^ (2 * (k + 1))) for i in range(nr)]))
        return out

    own_and_sends = [((cpd, nrhs), F32)] + [((cpd, nrhs), BF)] * (nz - 1)

    def k_coarse_faces(*refs):
        parts, (bf_ref, y_ref), faces = refs[:nz], refs[nz : nz + 2], refs[nz + 2 :]
        total = parts[0][...]
        for p in parts[1:]:
            total = total + p[...].astype(F32)
        y = total.astype(BF)
        y_ref[...] = y
        for s, ref in enumerate(faces):
            ref[...] = mm(bf_ref[pl.ds(s * ovl, ovl), :], y).astype(BF)

    def coarse_faces(parts):
        y, *faces = call(k_coarse_faces, [((cpd, nrhs), BF)] + [((ovl, nrhs), BF)] * 4, *parts, bfac)
        return y, faces

    def k_local(y_ref, base_ref, lb_ref, si_ref, bf_ref, *refs):
        olds, face_ref, wb = refs[:-2], refs[-2], refs[-1]
        y = y_ref[...]

        def tile(at):
            wb[at, :] = (base_ref[at, :] - mm(lb_ref[at, :], y)).astype(BF)

        row_loop(tile)
        for s in range(4):
            at = pl.ds(s * ovl, ovl)
            face = mm(bf_ref[at, :], y) + mm(si_ref[at, :], wb[...])
            face_ref[at, :] = face + olds[s][...].astype(F32) if olds else face

    def local(y, base, olds):
        (face,) = call(
            k_local, [((nf, nrhs), F32)], y, base, lbmat, simat, bfac, *olds,
            scratch=[pltpu.VMEM((nloc, nrhs), BF)], flops=2 * nf * nloc * nrhs,
        )
        return face

    def k_faces(base_ref, f_ref, *refs):
        recvs, faces = refs[:4], refs[4:]
        recv = jnp.concatenate([x[...] for x in recvs], axis=0)
        for s, ref in enumerate(faces):
            at = pl.ds(s * ovl, ovl)
            ref[...] = (base_ref[at, :] + mm(f_ref[at, :], recv)).astype(BF)

    def faces_after(base, recv):
        return call(k_faces, [((ovl, nrhs), BF)] * 4, base, fmat, *recv, flops=2 * nf * nf * nrhs)

    def k_advance(first, last, *refs):
        y_ref, base_ref, lb_ref, bt_ref, wt_ref, inv_ref, left_ref, right_ref = refs[:8]
        recvs, refs = refs[8:12], refs[12:]
        old_ref, refs = (None, refs) if first else (refs[0], refs[1:])
        out_ref, res_ref, wb, vb, recv = refs[:5]
        new_ref, sem = refs[5:] if last else (out_ref, None)
        y = y_ref[...]
        for s, x in enumerate(recvs):
            recv[pl.ds(s * ovl, ovl), :] = x[...]

        def base_tile(at):
            wb[at, :] = (base_ref[at, :] - mm(lb_ref[at, :], y) + mm(wt_ref[at, :], recv[...])).astype(BF)

        row_loop(base_tile)

        def sol_tile(at):
            new = mm(bt_ref[at, :], y) + mm(inv_ref[at, :], wb[...])
            if not first:
                new = new + old_ref[at, :]
            new_ref[at, :] = new
            vb[at, :] = new.astype(BF)

        row_loop(sol_tile)
        if last:
            store = pltpu.make_async_copy(new_ref, out_ref, sem)
            store.start()

            def res_tile(at):
                res_ref[at, :] = left_ref[at, :] - mm(right_ref[at, :], vb[...])

            row_loop(res_tile)
            store.wait()
        else:
            res_ref[...] = left_ref[...] - mm(right_ref[...], vb[...])

    def advance(y, base, recv, old, last, left, right):
        first = old is None
        outs = [((nloc, nrhs), F32), (left.shape, F32)]
        extra = [pltpu.VMEM((nloc, nrhs), F32), pltpu.SemaphoreType.DMA] if last else []
        return call(
            functools.partial(k_advance, first, last), outs,
            y, base, lbmat, btmat, wt, local_inv, left, right, *recv, *([] if first else [old]),
            scratch=[pltpu.VMEM((nloc, nrhs), BF)] * 2 + [pltpu.VMEM((nf, nrhs), BF)] + extra,
            hbm_outs=1 if last else 0, flops=5 * nloc * nloc * nrhs,
        )

    def k_restrict_recv(base_ref, t_ref, *refs):
        recvs, out_ref = refs[:4], refs[4]
        recv = jnp.concatenate([x[...] for x in recvs], axis=0)
        out_ref[...] = (base_ref[...] + mm(t_ref[...], recv)).astype(BF)

    def k_residual(sol_ref, mat_ref, rhs_ref, wt_ref, *refs):
        recvs, out_ref, recv, vb = refs[:4], refs[4], refs[5], refs[6]
        for s, x in enumerate(recvs):
            recv[pl.ds(s * ovl, ovl), :] = x[...]
        vb[...] = sol_ref[...].astype(BF)

        def tile(at):
            out_ref[at, :] = rhs_ref[at, :] - mm(mat_ref[at, :], vb[...]) + mm(wt_ref[at, :], recv[...])

        row_loop(tile)

    def residual_of(sol, recv):
        return call(
            k_residual, [((nloc, nrhs), F32)], sol, local_mat, rhs, wt, *recv,
            scratch=[pltpu.VMEM((nf, nrhs), BF), pltpu.VMEM((nloc, nrhs), BF)],
            flops=2 * nloc * (nloc + nf) * nrhs,
        )[0]

    def k_couple_last(res_ref, wt_ref, *refs):
        recvs, (out_ref, recv, buf, sems) = refs[:4], refs[4:]
        for s, x in enumerate(recvs):
            recv[pl.ds(s * ovl, ovl), :] = x[...]
        copies = []
        for i in range(nloc // last_step):
            at = pl.ds(i * last_step, last_step)
            buf[at, :] = res_ref[at, :] + mm(wt_ref[at, :], recv[...])
            copies.append(pltpu.make_async_copy(buf.at[at, :], out_ref.at[at, :], sems.at[i]))
            copies[-1].start()
        for copy in copies:
            copy.wait()

    def coupled(res, recv):
        return call(
            k_couple_last, [((nloc, nrhs), F32)], res, wt, *recv,
            scratch=[
                pltpu.VMEM((nf, nrhs), BF), pltpu.VMEM((nloc, nrhs), F32),
                pltpu.SemaphoreType.DMA((nloc // last_step,)),
            ],
            hbm_outs=1, flops=2 * nloc * nf * nrhs,
        )[0]

    def coarse_pair(mine, across, token):
        return call(
            k_coarse_pair, own_and_sends, *mine, *over_col(across), same, other, token,
            scratch=[pltpu.VMEM((nc * cpd, nrhs), BF)] * 2, tokens=1,
            flops=4 * half * nc * cpd * nrhs,
        )

    (lead,) = call(k_lead, [((8, 128), F32)], flops=8 * nloc * nloc * nrhs)
    restricted = mm(basis_t, rhs.astype(BF)).astype(BF)
    same, cross, restricted = call(
        k_hold, [((half, coarse_inv.shape[1]), BF)] * 2 + [((cpd, nrhs), BF)], coarse_inv, restricted, lead,
        tokens=1,
    )
    across = over_pair(restricted)
    other = over_pair(cross)
    mine = over_col(restricted)
    table = jnp.concatenate([margin_rows[0].astype(F32), couple[0]], axis=0)
    sel, wt, btmat = call(
        k_select, [((nf, nloc), BF), ((nloc, nf), BF), ((nloc, cpd), BF)], table, basis_t, restricted,
        tokens=1,
    )
    (lbmat,) = call(
        k_mat_basis, [((nloc, cpd), BF)], local_mat, btmat, wt, tokens=1,
        flops=2 * nloc * nloc * cpd,
    )
    own, *sends = coarse_pair(mine, across, lbmat)
    bfac, simat, fmat = call(
        k_products, [((nf, cpd), BF), ((nf, nloc), BF), ((nf, nf), BF)],
        sel, wt, local_inv, btmat, own, tokens=1, flops=2 * nf * nloc * (nloc + nf + cpd),
    )
    residual, solution, sent = rhs, None, []
    for sweep in range(STEPS):
        y, faces = coarse_faces(reduce_rows(own, sends))
        recv = halo(faces)
        if sweep == 0:
            zmat, tmat, brhs = call(
                k_restrictors, [((cpd, nloc), BF), ((cpd, nf), BF), ((cpd, nrhs), F32)],
                basis_t, local_mat, wt, rhs, y, tokens=1, flops=2 * cpd * nloc * (nloc + nf + nrhs),
            )
        sent = faces_after(local(y, residual, sent), recv)
        recv2 = halo(sent)
        if sweep == STEPS - 1:
            solution, res = advance(y, residual, recv, solution, True, rhs, local_mat)
            residual = coupled(res, recv2)
        else:
            solution, restr = advance(y, residual, recv, solution, False, brhs, zmat)
            (restricted,) = call(k_restrict_recv, [((cpd, nrhs), BF)], restr, tmat, *recv2)
            residual = residual_of(solution, recv2)
            own, *sends = coarse_pair(over_col(restricted), over_pair(restricted), residual)
    return (solution, residual)


def solution(mesh):
    nr, nc = mesh.shape["row"], mesh.shape["col"]
    placed = (
        P(("row", "col"), None),
        P(("row", "col"), None),
        P(("row", "col"), None),
        P(("row", "col"), None),
        P("col", "row"),
        P(("row", "col"), None, None),
        P(("row", "col"), None, None),
    )
    return jax.shard_map(
        functools.partial(per_device, nr, nc),
        mesh=mesh,
        in_specs=placed,
        out_specs=(P(("row", "col"), None), P(("row", "col"), None)),
        check_vma=False,
    )
```

```python
import functools

import jax
import jax.numpy as jnp
from jax import lax
from jax.experimental import pallas as pl
from jax.experimental.pallas import tpu as pltpu
from jax.sharding import PartitionSpec as P


BF = jnp.bfloat16
F32 = jnp.float32
VMEM = pl.BlockSpec(memory_space=pltpu.VMEM)
ANY = pl.BlockSpec(memory_space=pl.ANY)
LIMIT = 24 << 20


def mm(a, b):
    return jnp.dot(a, b, preferred_element_type=F32)


def call(kernel, outs, *args, scratch=(), flops=0, hbm_ins=0, hbm_outs=0, tokens=0):
    nbytes = sum(a.size * a.dtype.itemsize for a in args)
    inner = len(args) - hbm_ins - tokens
    return pl.pallas_call(
        kernel,
        out_shape=[jax.ShapeDtypeStruct(s, d) for s, d in outs],
        in_specs=[ANY] * hbm_ins + [VMEM] * inner + [ANY] * tokens,
        out_specs=[ANY] * hbm_outs + [VMEM] * (len(outs) - hbm_outs),
        scratch_shapes=list(scratch),
        compiler_params=pltpu.CompilerParams(vmem_limit_bytes=LIMIT),
        cost_estimate=pl.CostEstimate(flops=flops, bytes_accessed=nbytes, transcendentals=0),
    )(*args)


def tiles(rows, most=512):
    return most if rows % most == 0 else rows


def per_device(nr, nc, rhs, local_mat, local_inv, basis_t, coarse_inv, couple, margin_rows):
    nloc, nrhs = rhs.shape
    cpd = basis_t.shape[0]
    ovl = margin_rows.shape[2]
    nf = 4 * ovl
    nz = nr // 2
    both = ("row", "col")

    step, last_step = tiles(nloc), tiles(nloc, 256)

    def row_loop(body):
        @pl.loop(0, nloc // step)
        def _(i):
            body(pl.ds(pl.multiple_of(i * step, step), step))

    def pairs(row_parity, col_parity):
        perm = {}
        for r in range(nr):
            for c in range(nc):
                if row_parity is not None:
                    o = r + 1 if r % 2 == row_parity else r - 1
                    other = (o, c) if 0 <= o < nr else (r, c ^ 1)
                else:
                    o = c + 1 if c % 2 == col_parity else c - 1
                    other = (r, o) if 0 <= o < nc else (r, nc - 1 - c)
                perm[r * nc + c] = other[0] * nc + other[1]
        return sorted(perm.items())

    slot_perms = [pairs(1, None), pairs(None, 1), pairs(0, None), pairs(None, 0)]

    def slot_faces():
        r, c = lax.axis_index("row"), lax.axis_index("col")
        pr, pc = lax.rem(r, 2), lax.rem(c, 2)
        one = lambda ok: jnp.where(ok, 1.0, 0.0).astype(F32)
        return [
            (pr, one((pr == 1) & (r + 1 < nr) | (pr == 0) & (r > 0))),
            (2 + pc, one((pc == 1) & (c + 1 < nc) | (pc == 0) & (c > 0))),
            (1 - pr, one((pr == 1) | (r + 1 < nr))),
            (3 - pc, one((pc == 1) | (c + 1 < nc))),
        ]

    def halo(faces):
        out = []
        for f, p in zip(faces, slot_perms):
            out.append(lax.ppermute(f, both, p))
        return out

    def k_select(table_ref, basis_ref, token, sel_ref, wt_ref, bt_ref):
        bt_ref[...] = basis_ref[...].astype(F32).T.astype(BF)
        for s, (k, ok) in enumerate(slot_faces()):
            row = table_ref[pl.ds(k, 1), :].astype(jnp.int32)
            w = table_ref[pl.ds(4 + k, 1), :] * ok
            at = pl.ds(s * ovl, ovl)
            down = lax.broadcasted_iota(jnp.int32, (nloc, ovl), 0)
            wt_ref[:, at] = jnp.where(down == row, jnp.broadcast_to(w, (nloc, ovl)), 0.0).astype(BF)
            idx = jnp.broadcast_to(row.astype(F32), (ovl, ovl)).T
            for j in range(nloc // ovl):
                across = lax.broadcasted_iota(jnp.int32, (ovl, ovl), 1) + j * ovl
                sel_ref[at, pl.ds(j * ovl, ovl)] = jnp.where(idx == across.astype(F32), 1.0, 0.0).astype(BF)

    def k_products(sel_ref, wt_ref, inv_ref, bt_ref, token, bf_ref, si_ref, f_ref):
        bf_ref[...] = mm(sel_ref[...], bt_ref[...]).astype(BF)
        fstep = tiles(nf)

        @pl.loop(0, nf // fstep)
        def _(i):
            at = pl.ds(pl.multiple_of(i * fstep, fstep), fstep)
            si_ref[at, :] = mm(sel_ref[at, :], inv_ref[...]).astype(BF)
            f_ref[at, :] = mm(si_ref[at, :], wt_ref[...]).astype(BF)

    def k_mat_basis(mat_ref, bt_ref, token, lb_ref):
        def tile(at):
            lb_ref[at, :] = mm(mat_ref[at, :], bt_ref[...]).astype(BF)

        row_loop(tile)

    def k_restrictors(basis_ref, mat_ref, wt_ref, rhs_ref, token, z_ref, t_ref, brhs_ref):
        z_ref[...] = mm(basis_ref[...], mat_ref[...]).astype(BF)
        t_ref[...] = mm(basis_ref[...], wt_ref[...]).astype(BF)
        brhs_ref[...] = mm(basis_ref[...], rhs_ref[...].astype(BF))

    half = nz * cpd

    def k_lead(out_ref):
        out_ref[...] = jnp.zeros_like(out_ref)

    def k_hold(inv_ref, block_ref, token, same_ref, cross_ref, out_ref):
        r = lax.axis_index("row")
        out_ref[...] = block_ref[...]
        for i in range(nz):
            at = pl.ds(i * cpd, cpd)
            same_ref[at, :] = inv_ref[pl.ds(pl.multiple_of((r ^ (2 * i)) * cpd, 16), cpd), :]
            cross_ref[at, :] = inv_ref[pl.ds(pl.multiple_of((r ^ (2 * i + 1)) * cpd, 16), cpd), :]

    def place(group, blocks):
        c = lax.axis_index("col")
        for i, block in enumerate(blocks):
            group[pl.ds(pl.multiple_of((c ^ i) * cpd, 16), cpd), :] = block[...]

    def k_coarse_pair(*refs):
        mine, theirs, refs = refs[:nc], refs[nc : 2 * nc], refs[2 * nc :]
        same_ref, other_ref, _, own_ref = refs[:4]
        sends, (group, group_other) = refs[4:-2], refs[-2:]
        place(group, mine)
        place(group_other, theirs)
        for i, ref in enumerate((own_ref,) + tuple(sends)):
            at = pl.ds(i * cpd, cpd)
            ref[...] = (mm(same_ref[at, :], group[...]) + mm(other_ref[at, :], group_other[...])).astype(ref.dtype)

    def over_col(block):
        out = [block]
        for k in range(1, nc):
            out.append(lax.ppermute(block, "col", [(i, i ^ k) for i in range(nc)]))
        return out

    def over_pair(value):
        return lax.ppermute(value, "row", [(i, i ^ 1) for i in range(nr)])

    def reduce_rows(own, sends):
        out = [own]
        for k, block in enumerate(sends):
            out.append(lax.ppermute(block, "row", [(i, i ^ (2 * (k + 1))) for i in range(nr)]))
        return out

    own_and_sends = [((cpd, nrhs), F32)] + [((cpd, nrhs), BF)] * (nz - 1)

    def k_coarse_faces(*refs):
        parts, bf_ref, refs = refs[:nz], refs[nz], refs[-5:]
        y_ref, faces = refs[0], refs[1:]
        total = parts[0][...]
        for p in parts[1:]:
            total = total + p[...].astype(F32)
        y = total.astype(BF)
        y_ref[...] = y
        for s, ref in enumerate(faces):
            ref[...] = mm(bf_ref[pl.ds(s * ovl, ovl), :], y).astype(BF)

    def coarse_faces(parts, *tokens):
        y, *faces = call(
            k_coarse_faces, [((cpd, nrhs), BF)] + [((ovl, nrhs), BF)] * 4, *parts, bfac, *tokens,
            tokens=len(tokens),
        )
        return y, faces

    def k_local(y_ref, base_ref, lb_ref, si_ref, bf_ref, *refs):
        face_ref, wb = refs[-2:] if len(refs) == 2 else (refs[7], refs[9])
        y = y_ref[...]

        def tile(at):
            wb[at, :] = (base_ref[at, :] - mm(lb_ref[at, :], y)).astype(BF)

        row_loop(tile)
        for s in range(4):
            at = pl.ds(s * ovl, ovl)
            face = mm(bf_ref[at, :], y) + mm(si_ref[at, :], wb[...])
            face_ref[at, :] = face + refs[s][...].astype(F32) if len(refs) > 2 else face
        if len(refs) > 2:
            old_ref, bt_ref, inv_ref, pre_ref = refs[4:7] + refs[8:9]

            def pre_tile(at):
                pre_ref[at, :] = old_ref[at, :] + mm(bt_ref[at, :], y) + mm(inv_ref[at, :], wb[...])

            row_loop(pre_tile)

    def local(y, base, olds, old=None):
        more = [] if old is None else [*olds, old, btmat, local_inv]
        return call(
            k_local, [((nf, nrhs), F32)] + ([((nloc, nrhs), F32)] if more else []),
            y, base, lbmat, simat, bfac, *more,
            scratch=[pltpu.VMEM((nloc, nrhs), BF)], flops=2 * nf * nloc * nrhs,
        )

    def k_faces(base_ref, f_ref, *refs):
        recvs, faces = refs[:4], refs[4:]
        recv = jnp.concatenate([x[...] for x in recvs], axis=0)
        for s, ref in enumerate(faces):
            at = pl.ds(s * ovl, ovl)
            ref[...] = (base_ref[at, :] + mm(f_ref[at, :], recv)).astype(BF)

    def faces_after(base, recv):
        return call(k_faces, [((ovl, nrhs), BF)] * 4, base, fmat, *recv, flops=2 * nf * nf * nrhs)

    def k_advance(y_ref, base_ref, lb_ref, bt_ref, wt_ref, inv_ref, brhs_ref, z_ref, *refs):
        recvs, (new_ref, res_ref, wb, vb, recv) = refs[:4], refs[4:]
        y = y_ref[...]
        for s, x in enumerate(recvs):
            recv[pl.ds(s * ovl, ovl), :] = x[...]

        def base_tile(at):
            wb[at, :] = (base_ref[at, :] - mm(lb_ref[at, :], y) + mm(wt_ref[at, :], recv[...])).astype(BF)

        row_loop(base_tile)

        def sol_tile(at):
            new = mm(bt_ref[at, :], y) + mm(inv_ref[at, :], wb[...])
            new_ref[at, :] = new
            vb[at, :] = new.astype(BF)

        row_loop(sol_tile)
        res_ref[...] = brhs_ref[...] - mm(z_ref[...], vb[...])

    def advance(y, base, recv, brhs, zmat):
        return call(
            k_advance, [((nloc, nrhs), F32), (brhs.shape, F32)],
            y, base, lbmat, btmat, wt, local_inv, brhs, zmat, *recv,
            scratch=[pltpu.VMEM((nloc, nrhs), BF)] * 2 + [pltpu.VMEM((nf, nrhs), BF)],
            flops=5 * nloc * nloc * nrhs,
        )

    def k_finish(pre_ref, m_ref, rhs_ref, mat_ref, *refs):
        recvs, (out_ref, res_ref, vb, recv, new_ref, sem) = refs[:4], refs[4:]
        for s, x in enumerate(recvs):
            recv[pl.ds(s * ovl, ovl), :] = x[...]

        def sol_tile(at):
            new = pre_ref[at, :] + mm(m_ref[at, :], recv[...])
            new_ref[at, :] = new
            vb[at, :] = new.astype(BF)

        row_loop(sol_tile)
        store = pltpu.make_async_copy(new_ref, out_ref, sem)
        store.start()

        def res_tile(at):
            res_ref[at, :] = rhs_ref[at, :] - mm(mat_ref[at, :], vb[...])

        row_loop(res_tile)
        store.wait()

    def finish(pre, steer, recv):
        return call(
            k_finish, [((nloc, nrhs), F32)] * 2, pre, steer, rhs, local_mat, *recv,
            scratch=[
                pltpu.VMEM((nloc, nrhs), BF), pltpu.VMEM((nf, nrhs), BF),
                pltpu.VMEM((nloc, nrhs), F32), pltpu.SemaphoreType.DMA,
            ],
            hbm_outs=1, flops=2 * nloc * (nloc + nf) * nrhs,
        )

    def k_restrict_recv(base_ref, t_ref, *refs):
        recvs, out_ref = refs[:4], refs[4]
        recv = jnp.concatenate([x[...] for x in recvs], axis=0)
        out_ref[...] = (base_ref[...] + mm(t_ref[...], recv)).astype(BF)

    def k_residual(sol_ref, mat_ref, rhs_ref, wt_ref, *refs):
        recvs, out_ref, recv, vb = refs[:4], refs[4], refs[5], refs[6]
        for s, x in enumerate(recvs):
            recv[pl.ds(s * ovl, ovl), :] = x[...]
        vb[...] = sol_ref[...].astype(BF)

        def tile(at):
            out_ref[at, :] = rhs_ref[at, :] - mm(mat_ref[at, :], vb[...]) + mm(wt_ref[at, :], recv[...])

        row_loop(tile)

    def residual_of(sol, recv):
        return call(
            k_residual, [((nloc, nrhs), F32)], sol, local_mat, rhs, wt, *recv,
            scratch=[pltpu.VMEM((nf, nrhs), BF), pltpu.VMEM((nloc, nrhs), BF)],
            flops=2 * nloc * (nloc + nf) * nrhs,
        )[0]

    def k_couple_last(res_ref, wt_ref, *refs):
        recvs, (out_ref, recv, buf, sems) = refs[:4], refs[4:]
        for s, x in enumerate(recvs):
            recv[pl.ds(s * ovl, ovl), :] = x[...]
        copies = []
        for i in range(nloc // last_step):
            at = pl.ds(i * last_step, last_step)
            buf[at, :] = res_ref[at, :] + mm(wt_ref[at, :], recv[...])
            copies.append(pltpu.make_async_copy(buf.at[at, :], out_ref.at[at, :], sems.at[i]))
            copies[-1].start()
        for copy in copies:
            copy.wait()

    def coupled(res, recv):
        return call(
            k_couple_last, [((nloc, nrhs), F32)], res, wt, *recv,
            scratch=[
                pltpu.VMEM((nf, nrhs), BF), pltpu.VMEM((nloc, nrhs), F32),
                pltpu.SemaphoreType.DMA((nloc // last_step,)),
            ],
            hbm_outs=1, flops=2 * nloc * nf * nrhs,
        )[0]

    def coarse_pair(gathered, token):
        return call(
            k_coarse_pair, own_and_sends, *gathered, same, other, token,
            scratch=[pltpu.VMEM((nc * cpd, nrhs), BF)] * 2, tokens=1,
            flops=4 * half * nc * cpd * nrhs,
        )

    def k_steer(inv_ref, wt_ref, token, m_ref):
        def tile(at):
            m_ref[at, :] = mm(inv_ref[at, :], wt_ref[...]).astype(BF)

        row_loop(tile)

    (lead,) = call(k_lead, [((8, 128), F32)], flops=8 * nloc * nloc * nrhs)
    restricted = mm(basis_t, rhs.astype(BF)).astype(BF)
    same, cross, restricted = call(
        k_hold, [((half, coarse_inv.shape[1]), BF)] * 2 + [((cpd, nrhs), BF)], coarse_inv, restricted, lead,
        tokens=1,
    )
    across = over_pair(restricted)
    other = over_pair(cross)
    gathered = over_col(restricted) + over_col(across)
    table = jnp.concatenate([margin_rows[0].astype(F32), couple[0]], axis=0)
    sel, wt, btmat = call(
        k_select, [((nf, nloc), BF), ((nloc, nf), BF), ((nloc, cpd), BF)], table, basis_t, restricted,
        tokens=1,
    )
    (lbmat,) = call(
        k_mat_basis, [((nloc, cpd), BF)], local_mat, btmat, wt, tokens=1,
        flops=2 * nloc * nloc * cpd,
    )
    own, *sends = coarse_pair(gathered, lbmat)
    bfac, simat, fmat = call(
        k_products, [((nf, cpd), BF), ((nf, nloc), BF), ((nf, nf), BF)],
        sel, wt, local_inv, btmat, own, tokens=1, flops=2 * nf * nloc * (nloc + nf + cpd),
    )
    y, faces = coarse_faces(reduce_rows(own, sends))
    recv = halo(faces)
    zmat, tmat, brhs = call(
        k_restrictors, [((cpd, nloc), BF), ((cpd, nf), BF), ((cpd, nrhs), F32)],
        basis_t, local_mat, wt, rhs, y, tokens=1, flops=2 * cpd * nloc * (nloc + nf + nrhs),
    )
    (face_base,) = local(y, rhs, [])
    sent = faces_after(face_base, recv)
    recv2 = halo(sent)
    solution, restr = advance(y, rhs, recv, brhs, zmat)
    (restricted,) = call(k_restrict_recv, [((cpd, nrhs), BF)], restr, tmat, *recv2)
    across = over_pair(restricted)
    gathered = over_col(restricted) + over_col(across)
    residual = residual_of(solution, recv2)
    own, *sends = coarse_pair(gathered, residual)
    (steer,) = call(k_steer, [((nloc, nf), BF)], local_inv, wt, own, tokens=1, flops=2 * nloc * nloc * nf)
    y, faces = coarse_faces(reduce_rows(own, sends), steer)
    recv = halo(faces)
    face_base, before = local(y, residual, sent, solution)
    sent = faces_after(face_base, recv)
    recv2 = halo(sent)
    solution, res = finish(before, steer, recv)
    residual = coupled(res, recv2)
    return (solution, residual)


def solution(mesh):
    nr, nc = mesh.shape["row"], mesh.shape["col"]
    placed = (
        P(("row", "col"), None),
        P(("row", "col"), None),
        P(("row", "col"), None),
        P(("row", "col"), None),
        P("col", "row"),
        P(("row", "col"), None, None),
        P(("row", "col"), None, None),
    )
    return jax.shard_map(
        functools.partial(per_device, nr, nc),
        mesh=mesh,
        in_specs=placed,
        out_specs=(P(("row", "col"), None), P(("row", "col"), None)),
        check_vma=False,
    )
```

```python
import functools

import jax
import jax.numpy as jnp
from jax import lax
from jax.experimental import pallas as pl
from jax.experimental.pallas import tpu as pltpu
from jax.sharding import PartitionSpec as P


BF = jnp.bfloat16
F32 = jnp.float32
VMEM = pl.BlockSpec(memory_space=pltpu.VMEM)
ANY = pl.BlockSpec(memory_space=pl.ANY)
LIMIT = 24 << 20


def mm(a, b):
    return jnp.dot(a, b, preferred_element_type=F32)


def call(kernel, outs, *args, scratch=(), flops=0, hbm_ins=0, hbm_outs=0, tokens=0):
    nbytes = sum(a.size * a.dtype.itemsize for a in args)
    inner = len(args) - hbm_ins - tokens
    return pl.pallas_call(
        kernel,
        out_shape=[jax.ShapeDtypeStruct(s, d) for s, d in outs],
        in_specs=[ANY] * hbm_ins + [VMEM] * inner + [ANY] * tokens,
        out_specs=[ANY] * hbm_outs + [VMEM] * (len(outs) - hbm_outs),
        scratch_shapes=list(scratch),
        compiler_params=pltpu.CompilerParams(vmem_limit_bytes=LIMIT),
        cost_estimate=pl.CostEstimate(flops=flops, bytes_accessed=nbytes, transcendentals=0),
    )(*args)


def tiles(rows, most=512):
    return most if rows % most == 0 else rows


def per_device(nr, nc, rhs, local_mat, local_inv, basis_t, coarse_inv, couple, margin_rows):
    nloc, nrhs = rhs.shape
    cpd = basis_t.shape[0]
    ovl = margin_rows.shape[2]
    nf = 4 * ovl
    nz = nr // 2
    both = ("row", "col")

    step, last_step = tiles(nloc), tiles(nloc, 256)

    def row_loop(body):
        @pl.loop(0, nloc // step)
        def _(i):
            body(pl.ds(pl.multiple_of(i * step, step), step))

    def pairs(row_parity, col_parity):
        perm = {}
        for r in range(nr):
            for c in range(nc):
                if row_parity is not None:
                    o = r + 1 if r % 2 == row_parity else r - 1
                    other = (o, c) if 0 <= o < nr else (r, c ^ 1)
                else:
                    o = c + 1 if c % 2 == col_parity else c - 1
                    other = (r, o) if 0 <= o < nc else (r, nc - 1 - c)
                perm[r * nc + c] = other[0] * nc + other[1]
        return sorted(perm.items())

    slot_perms = [pairs(1, None), pairs(None, 1), pairs(0, None), pairs(None, 0)]

    def slot_faces():
        r, c = lax.axis_index("row"), lax.axis_index("col")
        pr, pc = lax.rem(r, 2), lax.rem(c, 2)
        one = lambda ok: jnp.where(ok, 1.0, 0.0).astype(F32)
        return [
            (pr, one((pr == 1) & (r + 1 < nr) | (pr == 0) & (r > 0))),
            (2 + pc, one((pc == 1) & (c + 1 < nc) | (pc == 0) & (c > 0))),
            (1 - pr, one((pr == 1) | (r + 1 < nr))),
            (3 - pc, one((pc == 1) | (c + 1 < nc))),
        ]

    def halo(faces):
        out = []
        for f, p in zip(faces, slot_perms):
            out.append(lax.ppermute(f, both, p))
        return out

    def k_select(table_ref, basis_ref, token, sel_ref, wt_ref, bt_ref):
        bt_ref[...] = basis_ref[...].astype(F32).T.astype(BF)
        for s, (k, ok) in enumerate(slot_faces()):
            row = table_ref[pl.ds(k, 1), :].astype(jnp.int32)
            w = table_ref[pl.ds(4 + k, 1), :] * ok
            at = pl.ds(s * ovl, ovl)
            down = lax.broadcasted_iota(jnp.int32, (nloc, ovl), 0)
            wt_ref[:, at] = jnp.where(down == row, jnp.broadcast_to(w, (nloc, ovl)), 0.0).astype(BF)
            idx = jnp.broadcast_to(row.astype(F32), (ovl, ovl)).T
            for j in range(nloc // ovl):
                across = lax.broadcasted_iota(jnp.int32, (ovl, ovl), 1) + j * ovl
                sel_ref[at, pl.ds(j * ovl, ovl)] = jnp.where(idx == across.astype(F32), 1.0, 0.0).astype(BF)

    def k_products(sel_ref, wt_ref, inv_ref, bt_ref, token, bf_ref, si_ref, f_ref):
        bf_ref[...] = mm(sel_ref[...], bt_ref[...]).astype(BF)
        fstep = tiles(nf)

        @pl.loop(0, nf // fstep)
        def _(i):
            at = pl.ds(pl.multiple_of(i * fstep, fstep), fstep)
            si_ref[at, :] = mm(sel_ref[at, :], inv_ref[...]).astype(BF)
            f_ref[at, :] = mm(si_ref[at, :], wt_ref[...]).astype(BF)

    def k_mat_basis(mat_ref, bt_ref, token, lb_ref):
        def tile(at):
            lb_ref[at, :] = mm(mat_ref[at, :], bt_ref[...]).astype(BF)

        row_loop(tile)

    def k_restrictors(basis_ref, mat_ref, wt_ref, rhs_ref, token, z_ref, t_ref, brhs_ref):
        z_ref[...] = mm(basis_ref[...], mat_ref[...]).astype(BF)
        t_ref[...] = mm(basis_ref[...], wt_ref[...]).astype(BF)
        brhs_ref[...] = mm(basis_ref[...], rhs_ref[...].astype(BF))

    half = nz * cpd

    def k_lead(out_ref):
        out_ref[...] = jnp.zeros_like(out_ref)

    def k_hold(inv_ref, block_ref, token, same_ref, cross_ref, out_ref):
        r = lax.axis_index("row")
        out_ref[...] = block_ref[...]
        for i in range(nz):
            at = pl.ds(i * cpd, cpd)
            same_ref[at, :] = inv_ref[pl.ds(pl.multiple_of((r ^ (2 * i)) * cpd, 16), cpd), :]
            cross_ref[at, :] = inv_ref[pl.ds(pl.multiple_of((r ^ (2 * i + 1)) * cpd, 16), cpd), :]

    def place(group, blocks):
        c = lax.axis_index("col")
        for i, block in enumerate(blocks):
            group[pl.ds(pl.multiple_of((c ^ i) * cpd, 16), cpd), :] = block[...]

    def k_coarse_pair(*refs):
        mine, theirs, refs = refs[:nc], refs[nc : 2 * nc], refs[2 * nc :]
        same_ref, other_ref, _, own_ref = refs[:4]
        sends, (group, group_other) = refs[4:-2], refs[-2:]
        place(group, mine)
        place(group_other, theirs)
        total = mm(same_ref[...], group[...]) + mm(other_ref[...], group_other[...])
        for i, ref in enumerate((own_ref,) + tuple(sends)):
            ref[...] = total[i * cpd : (i + 1) * cpd].astype(ref.dtype)

    def over_col(block):
        out = [block]
        for k in range(1, nc):
            out.append(lax.ppermute(block, "col", [(i, i ^ k) for i in range(nc)]))
        return out

    def over_pair(value):
        return lax.ppermute(value, "row", [(i, i ^ 1) for i in range(nr)])

    def reduce_rows(own, sends):
        out = [own]
        for k, block in enumerate(sends):
            out.append(lax.ppermute(block, "row", [(i, i ^ (2 * (k + 1))) for i in range(nr)]))
        return out

    own_and_sends = [((cpd, nrhs), F32)] + [((cpd, nrhs), BF)] * (nz - 1)

    def k_coarse_faces(*refs):
        parts, bf_ref, refs = refs[:nz], refs[nz], refs[-5:]
        y_ref, faces = refs[0], refs[1:]
        total = parts[0][...]
        for p in parts[1:]:
            total = total + p[...].astype(F32)
        y = total.astype(BF)
        y_ref[...] = y
        total = mm(bf_ref[...], y)
        for s, ref in enumerate(faces):
            ref[...] = total[s * ovl : (s + 1) * ovl].astype(BF)

    def coarse_faces(parts, *tokens):
        y, *faces = call(
            k_coarse_faces, [((cpd, nrhs), BF)] + [((ovl, nrhs), BF)] * 4, *parts, bfac, *tokens,
            tokens=len(tokens),
        )
        return y, faces

    def k_local(y_ref, base_ref, lb_ref, si_ref, bf_ref, *refs):
        face_ref, wb = refs[-2:] if len(refs) == 2 else (refs[7], refs[9])
        y = y_ref[...]

        def tile(at):
            wb[at, :] = (base_ref[at, :] - mm(lb_ref[at, :], y)).astype(BF)

        row_loop(tile)
        face = mm(bf_ref[...], y) + mm(si_ref[...], wb[...])
        for s in range(4):
            at = pl.ds(s * ovl, ovl)
            part = face[s * ovl : (s + 1) * ovl]
            face_ref[at, :] = part + refs[s][...].astype(F32) if len(refs) > 2 else part
        if len(refs) > 2:
            old_ref, bt_ref, inv_ref, pre_ref = refs[4:7] + refs[8:9]

            def pre_tile(at):
                pre_ref[at, :] = old_ref[at, :] + mm(bt_ref[at, :], y) + mm(inv_ref[at, :], wb[...])

            row_loop(pre_tile)

    def local(y, base, olds, old=None):
        more = [] if old is None else [*olds, old, btmat, local_inv]
        return call(
            k_local, [((nf, nrhs), F32)] + ([((nloc, nrhs), F32)] if more else []),
            y, base, lbmat, simat, bfac, *more,
            scratch=[pltpu.VMEM((nloc, nrhs), BF)], flops=2 * nf * nloc * nrhs,
        )

    def k_faces(base_ref, f_ref, *refs):
        recvs, faces = refs[:4], refs[4:]
        recv = jnp.concatenate([x[...] for x in recvs], axis=0)
        total = base_ref[...] + mm(f_ref[...], recv)
        for s, ref in enumerate(faces):
            ref[...] = total[s * ovl : (s + 1) * ovl].astype(BF)

    def faces_after(base, recv):
        return call(k_faces, [((ovl, nrhs), BF)] * 4, base, fmat, *recv, flops=2 * nf * nf * nrhs)

    def k_advance(y_ref, base_ref, lb_ref, bt_ref, wt_ref, inv_ref, brhs_ref, z_ref, *refs):
        recvs, (new_ref, res_ref, wb, vb, recv) = refs[:4], refs[4:]
        y = y_ref[...]
        for s, x in enumerate(recvs):
            recv[pl.ds(s * ovl, ovl), :] = x[...]

        def base_tile(at):
            wb[at, :] = (base_ref[at, :] - mm(lb_ref[at, :], y) + mm(wt_ref[at, :], recv[...])).astype(BF)

        base_tile(pl.ds(0, nloc))

        def sol_tile(at):
            new = mm(bt_ref[at, :], y) + mm(inv_ref[at, :], wb[...])
            new_ref[at, :] = new
            vb[at, :] = new.astype(BF)

        row_loop(sol_tile)
        res_ref[...] = brhs_ref[...] - mm(z_ref[...], vb[...])

    def advance(y, base, recv, brhs, zmat):
        return call(
            k_advance, [((nloc, nrhs), F32), (brhs.shape, F32)],
            y, base, lbmat, btmat, wt, local_inv, brhs, zmat, *recv,
            scratch=[pltpu.VMEM((nloc, nrhs), BF)] * 2 + [pltpu.VMEM((nf, nrhs), BF)],
            flops=5 * nloc * nloc * nrhs,
        )

    def k_finish(pre_ref, m_ref, rhs_ref, mat_ref, *refs):
        recvs, (out_ref, res_ref, vb, recv, new_ref, sem) = refs[:4], refs[4:]
        for s, x in enumerate(recvs):
            recv[pl.ds(s * ovl, ovl), :] = x[...]

        def sol_tile(at):
            new = pre_ref[at, :] + mm(m_ref[at, :], recv[...])
            new_ref[at, :] = new
            vb[at, :] = new.astype(BF)

        row_loop(sol_tile)
        store = pltpu.make_async_copy(new_ref, out_ref, sem)
        store.start()

        def res_tile(at):
            res_ref[at, :] = rhs_ref[at, :] - mm(mat_ref[at, :], vb[...])

        row_loop(res_tile)
        store.wait()

    def finish(pre, steer, recv):
        return call(
            k_finish, [((nloc, nrhs), F32)] * 2, pre, steer, rhs, local_mat, *recv,
            scratch=[
                pltpu.VMEM((nloc, nrhs), BF), pltpu.VMEM((nf, nrhs), BF),
                pltpu.VMEM((nloc, nrhs), F32), pltpu.SemaphoreType.DMA,
            ],
            hbm_outs=1, flops=2 * nloc * (nloc + nf) * nrhs,
        )

    def k_restrict_recv(base_ref, t_ref, *refs):
        recvs, out_ref = refs[:4], refs[4]
        recv = jnp.concatenate([x[...] for x in recvs], axis=0)
        out_ref[...] = (base_ref[...] + mm(t_ref[...], recv)).astype(BF)

    def k_residual(sol_ref, mat_ref, rhs_ref, wt_ref, *refs):
        recvs, out_ref, recv, vb = refs[:4], refs[4], refs[5], refs[6]
        for s, x in enumerate(recvs):
            recv[pl.ds(s * ovl, ovl), :] = x[...]
        vb[...] = sol_ref[...].astype(BF)

        def tile(at):
            out_ref[at, :] = rhs_ref[at, :] - mm(mat_ref[at, :], vb[...]) + mm(wt_ref[at, :], recv[...])

        row_loop(tile)

    def residual_of(sol, recv):
        return call(
            k_residual, [((nloc, nrhs), F32)], sol, local_mat, rhs, wt, *recv,
            scratch=[pltpu.VMEM((nf, nrhs), BF), pltpu.VMEM((nloc, nrhs), BF)],
            flops=2 * nloc * (nloc + nf) * nrhs,
        )[0]

    def k_couple_last(res_ref, wt_ref, *refs):
        recvs, (out_ref, recv, buf, sems) = refs[:4], refs[4:]
        for s, x in enumerate(recvs):
            recv[pl.ds(s * ovl, ovl), :] = x[...]
        copies = []
        for i in range(nloc // last_step):
            at = pl.ds(i * last_step, last_step)
            buf[at, :] = res_ref[at, :] + mm(wt_ref[at, :], recv[...])
            copies.append(pltpu.make_async_copy(buf.at[at, :], out_ref.at[at, :], sems.at[i]))
            copies[-1].start()
        for copy in copies:
            copy.wait()

    def coupled(res, recv):
        return call(
            k_couple_last, [((nloc, nrhs), F32)], res, wt, *recv,
            scratch=[
                pltpu.VMEM((nf, nrhs), BF), pltpu.VMEM((nloc, nrhs), F32),
                pltpu.SemaphoreType.DMA((nloc // last_step,)),
            ],
            hbm_outs=1, flops=2 * nloc * nf * nrhs,
        )[0]

    def coarse_pair(gathered, token):
        return call(
            k_coarse_pair, own_and_sends, *gathered, same, other, token,
            scratch=[pltpu.VMEM((nc * cpd, nrhs), BF)] * 2, tokens=1,
            flops=4 * half * nc * cpd * nrhs,
        )

    def k_steer(inv_ref, wt_ref, token, m_ref):
        def tile(at):
            m_ref[at, :] = mm(inv_ref[at, :], wt_ref[...]).astype(BF)

        row_loop(tile)

    (lead,) = call(k_lead, [((8, 128), F32)], flops=8 * nloc * nloc * nrhs)
    restricted = mm(basis_t, rhs.astype(BF)).astype(BF)
    same, cross, restricted = call(
        k_hold, [((half, coarse_inv.shape[1]), BF)] * 2 + [((cpd, nrhs), BF)], coarse_inv, restricted, lead,
        tokens=1,
    )
    across = over_pair(restricted)
    other = over_pair(cross)
    gathered = over_col(restricted) + over_col(across)
    table = jnp.concatenate([margin_rows[0].astype(F32), couple[0]], axis=0)
    sel, wt, btmat = call(
        k_select, [((nf, nloc), BF), ((nloc, nf), BF), ((nloc, cpd), BF)], table, basis_t, restricted,
        tokens=1,
    )
    (lbmat,) = call(
        k_mat_basis, [((nloc, cpd), BF)], local_mat, btmat, wt, tokens=1,
        flops=2 * nloc * nloc * cpd,
    )
    own, *sends = coarse_pair(gathered, lbmat)
    bfac, simat, fmat = call(
        k_products, [((nf, cpd), BF), ((nf, nloc), BF), ((nf, nf), BF)],
        sel, wt, local_inv, btmat, own, tokens=1, flops=2 * nf * nloc * (nloc + nf + cpd),
    )
    y, faces = coarse_faces(reduce_rows(own, sends))
    recv = halo(faces)
    zmat, tmat, brhs = call(
        k_restrictors, [((cpd, nloc), BF), ((cpd, nf), BF), ((cpd, nrhs), F32)],
        basis_t, local_mat, wt, rhs, y, tokens=1, flops=2 * cpd * nloc * (nloc + nf + nrhs),
    )
    (face_base,) = local(y, rhs, [])
    sent = faces_after(face_base, recv)
    recv2 = halo(sent)
    solution, restr = advance(y, rhs, recv, brhs, zmat)
    (restricted,) = call(k_restrict_recv, [((cpd, nrhs), BF)], restr, tmat, *recv2)
    across = over_pair(restricted)
    gathered = over_col(restricted) + over_col(across)
    residual = residual_of(solution, recv2)
    own, *sends = coarse_pair(gathered, residual)
    (steer,) = call(k_steer, [((nloc, nf), BF)], local_inv, wt, own, tokens=1, flops=2 * nloc * nloc * nf)
    y, faces = coarse_faces(reduce_rows(own, sends), steer)
    recv = halo(faces)
    face_base, before = local(y, residual, sent, solution)
    sent = faces_after(face_base, recv)
    recv2 = halo(sent)
    solution, res = finish(before, steer, recv)
    residual = coupled(res, recv2)
    return (solution, residual)


def solution(mesh):
    nr, nc = mesh.shape["row"], mesh.shape["col"]
    placed = (
        P(("row", "col"), None),
        P(("row", "col"), None),
        P(("row", "col"), None),
        P(("row", "col"), None),
        P("col", "row"),
        P(("row", "col"), None, None),
        P(("row", "col"), None, None),
    )
    return jax.shard_map(
        functools.partial(per_device, nr, nc),
        mesh=mesh,
        in_specs=placed,
        out_specs=(P(("row", "col"), None), P(("row", "col"), None)),
        check_vma=False,
    )
```
